32 devices in a mesh: tile: 8 (over z, y), mem: 4 (over x, core).
Axes of the slice: x: 2, y: 2, z: 4, core: 2. Of those that a mesh axis runs over, the one named last changes fastest.
Arguments:
- control: bfloat16 [32, 16, 24576], P('mem', None, 'tile'), may hold values from -6 to 6
- ensemble: bfloat16 [32, 16, 24576], P('mem', None, 'tile'), may hold values from -1 to 1
- vertical_loc: bfloat16 [16, 16], replicated, may hold values from -1.5 to 1.5
- blocks: bfloat16 [192, 7, 128, 128], P('tile'), as said below
- edge_mask: int32 [192, 7], P('tile'), may hold values from 0 to 1, as said below
- background: float32 [16, 24576], P(None, 'tile'), may hold values from -6 to 6
- obs_precision: float32 [16, 24576], P(None, 'tile'), may hold values from 1 to 10
Outputs:
- increment: float32 [16, 24576], P('mem', 'tile')
- gradient: float32 [32, 16, 24576], P('mem', None, 'tile')
The draws below stay inside these ranges and needn't reach their ends.
Inputs may be any that keep to these rules, and one draw needn't show every extreme that they name: `edge_mask`: each entry is 0 or 1; slot 0 is 1 for every tile; slot 2d of tile (t + d) mod 192 equals slot 2d-1 of tile t. Slot 0 blocks are symmetric, and the block in slot 2d of tile (t + d) mod 192 is the transpose of the block in slot 2d-1 of tile t, so that Lh is symmetric.
All inputs are finite; a program needn't handle non-finite values.
Results may differ from the reference program's by a relative error of at most 0.011.
Values may be sent and summed in bfloat16 or wider, within the bound.
No kernel may reach another device: no remote copies, remote signals or barrier semaphores. Data moves between devices by JAX's collectives and lax.ppermute only.
A program may use at most 64 MiB of HBM per device.

```python
import math
import jax
import jax.numpy as jnp
from jax import lax

BLK = 128
LEV = 16
REACH = 3
KB = 7
MEMBERS = 32
NT = 192
NH = 24576


def draw_blocks(key, part):
    block_key = jax.random.fold_in(key, 11)
    block_scale = 1.0 / math.sqrt(BLK * KB)
    random_part = jax.random.normal(block_key, (NT, REACH + 1, BLK, BLK), jnp.float32)
    random_part = random_part * block_scale
    identity = jnp.eye(BLK, dtype=jnp.float32)
    self_block = (random_part[:, 0] + jnp.swapaxes(random_part[:, 0], -1, -2)) / math.sqrt(2.0) + identity[None]
    pieces = [self_block]
    for distance in range(1, REACH + 1):
        forward_block = random_part[:, distance]
        backward_block = jnp.swapaxes(jnp.roll(random_part[:, distance], distance, axis=0), -1, -2)
        pieces.append(forward_block)
        pieces.append(backward_block)
    return jnp.stack(pieces, axis=1).astype(jnp.bfloat16)


def draw_edge_mask(key, part):
    edge_key = jax.random.fold_in(key, 7)
    edge_bits = jax.random.randint(edge_key, (NT, REACH), 0, 2, dtype=jnp.int32)
    pieces = [jnp.ones((NT,), jnp.int32)]
    for distance in range(1, REACH + 1):
        pieces.append(edge_bits[:, distance - 1])
        pieces.append(jnp.roll(edge_bits[:, distance - 1], distance, axis=0))
    return jnp.stack(pieces, axis=1).astype(jnp.int32)


def levels(key, extent, cuts, smallest, high):
    loudness, own = 1.0, jax.random.fold_in(key, 6)
    for axis_at, parts in cuts:
        steps = jnp.exp(jax.random.uniform(jax.random.fold_in(own, axis_at), (parts,), jnp.float32, smallest / len(cuts), high / len(cuts)))
        loudness = loudness * jnp.repeat(steps, extent[axis_at] // parts).reshape([-1 if axis == axis_at else 1 for axis in range(len(extent))])
    return loudness


def centred(own_key, dims, deviation, reach, split=(), kind=jnp.bfloat16):
    entries = jax.random.normal(own_key, dims, jnp.float32) * deviation
    if len(split) > 0:
        entries = levels(own_key, dims, split, -0.22, 0.18) * entries
    return jnp.clip(entries, min=-reach, max=reach).astype(kind)


def setup_inputs(seed: int = 0) -> dict:
    key_list = jax.random.split(jax.random.key(seed), 8)
    control = centred(key_list[0], (MEMBERS, LEV, NH), 1.0, 6.0, ((0, 4), (2, 8)))
    ensemble = centred(key_list[1], (MEMBERS, LEV, NH), MEMBERS ** -0.5, 1.0, ((0, 4), (2, 8)))
    vertical_loc = centred(key_list[2], (LEV, LEV), LEV ** -0.5, 1.5)
    blocks = draw_blocks(jax.random.fold_in(key_list[7], 71), 0)
    edge_mask = draw_edge_mask(jax.random.fold_in(key_list[7], 71), 0)
    background = centred(key_list[5], (LEV, NH), 1.0, 6.0, ((1, 8),), jnp.float32)
    obs_precision = jnp.clip(jnp.exp(math.log(10.0) - 2.3025851 * jax.random.uniform(key_list[6], (LEV, NH), jnp.float32) ** levels(key_list[6], (LEV, NH), ((1, 8),), -0.2, 0.2)), 1.0, 10.0)
    return dict(control=control, ensemble=ensemble, vertical_loc=vertical_loc, blocks=blocks, edge_mask=edge_mask, background=background, obs_precision=obs_precision)


def slot_offset(slot_index):
    if slot_index == 0:
        return 0
    distance = (slot_index + 1) // 2
    if slot_index % 2 == 1:
        return distance
    return -distance


def reference(control, ensemble, vertical_loc, blocks, edge_mask, background, obs_precision):
    member_count, level_count, point_count = control.shape
    tile_count = point_count // BLK
    mask_float = edge_mask.astype(jnp.float32)
    blocks_float = blocks.astype(jnp.float32)
    loc_float = vertical_loc.astype(jnp.float32)
    vertical = jnp.einsum('lm,kmh->klh', loc_float, control.astype(jnp.float32)).astype(jnp.bfloat16)
    vertical_tiles = vertical.astype(jnp.float32).reshape(member_count, level_count, tile_count, BLK)
    localized = jnp.zeros(vertical_tiles.shape, jnp.float32)
    for slot_index in range(KB):
        offset = slot_offset(slot_index)
        source = jnp.roll(vertical_tiles, -offset, axis=2)
        product = jnp.einsum('tab,kltb->klta', blocks_float[:, slot_index], source)
        localized = localized + mask_float[None, None, :, slot_index, None] * product
    localized = localized.reshape(member_count, level_count, point_count)
    increment = jnp.sum(ensemble.astype(jnp.float32) * localized, axis=0)
    depart = (obs_precision * (increment - background)).astype(jnp.bfloat16)
    weighted = (ensemble.astype(jnp.float32) * depart.astype(jnp.float32)[None]).astype(jnp.bfloat16)
    weighted_tiles = weighted.astype(jnp.float32).reshape(member_count, level_count, tile_count, BLK)
    adjoint = jnp.zeros(weighted_tiles.shape, jnp.float32)
    for slot_index in range(KB):
        offset = slot_offset(slot_index)
        contrib = jnp.einsum('tab,klta->kltb', blocks_float[:, slot_index], weighted_tiles)
        contrib = mask_float[None, None, :, slot_index, None] * contrib
        adjoint = adjoint + jnp.roll(contrib, offset, axis=2)
    adjoint = adjoint.reshape(member_count, level_count, point_count)
    gradient = control.astype(jnp.float32) + jnp.einsum('ml,kmh->klh', loc_float, adjoint, precision=lax.Precision.HIGHEST)
    return increment, gradient
```

```python
import jax
import jax.numpy as jnp
from jax import lax
from jax.experimental import pallas as pl
from jax.experimental.pallas import tpu as pltpu
from jax.sharding import PartitionSpec as P


def slot_offset(slot_index):
    distance = (slot_index + 1) // 2
    return distance if slot_index % 2 == 1 else -distance


def slot_order(slot_count):
    return sorted(range(slot_count), key=slot_offset)


def spread(loc, rows):
    levels = loc.shape[0]
    pick = (
        lax.broadcasted_iota(jnp.int32, (rows, levels), 0) % levels
        == lax.broadcasted_iota(jnp.int32, (rows, levels), 1)
    ).astype(jnp.bfloat16)
    tall = jnp.dot(pick, loc, preferred_element_type=jnp.float32).astype(jnp.bfloat16)
    wide = lax.dot_general(
        tall, pick, (((1,), (1,)), ((), ())), preferred_element_type=jnp.float32
    )
    same = (
        lax.broadcasted_iota(jnp.int32, (rows, rows), 0) // levels
        == lax.broadcasted_iota(jnp.int32, (rows, rows), 1) // levels
    )
    return jnp.where(same, wide, 0.0).astype(jnp.bfloat16)


def tile_row(field_ref, blocks_ref, mask_ref, tile):
    slots, width = blocks_ref.shape[1], blocks_ref.shape[2]
    parts = []
    for slot in slot_order(slots):
        block = blocks_ref[tile, slot]
        keep = mask_ref[tile, slot].astype(jnp.float32).astype(jnp.bfloat16)
        parts.append(block * keep)
    row = jnp.concatenate(parts, axis=1)
    start = pl.multiple_of(tile * width, width)
    source = field_ref[:, pl.ds(start, slots * width)]
    return lax.dot_general(
        source, row, (((1,), (1,)), ((), ())), preferred_element_type=jnp.float32
    )


def forward_kernel(even_ref, mask_ref, loc_ref, control_ref, near_ref, far_ref, ensemble_ref,
                   blocks_ref, partial_ref, field_ref):
    members, levels, points = control_ref.shape
    rows, width = members * levels, blocks_ref.shape[2]
    rim = near_ref.shape[2]
    up = spread(loc_ref[...], rows)

    def vertical(value):
        return jnp.dot(
            up, value.reshape(rows, value.shape[2]), preferred_element_type=jnp.float32
        ).astype(jnp.bfloat16)

    even = even_ref[0]
    near_at = pl.multiple_of(even * (points + rim), width)
    far_at = pl.multiple_of((1 - even) * (points + rim), width)
    field_ref[:, pl.ds(near_at, rim)] = vertical(near_ref[...])
    field_ref[:, pl.ds(far_at, rim)] = vertical(far_ref[...])
    field_ref[:, rim : rim + points] = vertical(control_ref[...])

    def step(tile, carry):
        localized = tile_row(field_ref, blocks_ref, mask_ref, tile)
        at = pl.multiple_of(tile * width, width)
        weight = ensemble_ref[:, :, pl.ds(at, width)].astype(jnp.float32)
        total = jnp.sum(weight * localized.reshape(members, levels, width), axis=0)
        partial_ref[:, pl.ds(at, width)] = total.astype(jnp.bfloat16)
        return carry

    lax.fori_loop(0, points // width, step, 0, unroll=4)


def backward_kernel(even_ref, mask_ref, loc_ref, control_ref, depart_ref, depart_near_ref,
                    depart_far_ref, ensemble_ref, near_ref, far_ref, blocks_ref, gradient_ref,
                    field_ref):
    members, levels, points = control_ref.shape
    rows, width = members * levels, blocks_ref.shape[2]
    rim = near_ref.shape[2]
    down = spread(loc_ref[...].T, rows)

    def weighted(value, depart):
        product = value.astype(jnp.float32) * depart.astype(jnp.float32)[None]
        return product.astype(jnp.bfloat16).reshape(rows, value.shape[2])

    even = even_ref[0]
    near_at = pl.multiple_of(even * (points + rim), width)
    far_at = pl.multiple_of((1 - even) * (points + rim), width)
    field_ref[:, pl.ds(near_at, rim)] = weighted(near_ref[...], depart_near_ref[...])
    field_ref[:, pl.ds(far_at, rim)] = weighted(far_ref[...], depart_far_ref[...])
    field_ref[:, rim : rim + points] = weighted(ensemble_ref[...], depart_ref[...])

    def step(tile, carry):
        adjoint = tile_row(field_ref, blocks_ref, mask_ref, tile).astype(jnp.bfloat16)
        at = pl.multiple_of(tile * width, width)
        change = jnp.dot(down, adjoint, preferred_element_type=jnp.float32)
        gradient_ref[:, :, pl.ds(at, width)] = control_ref[:, :, pl.ds(at, width)].astype(
            jnp.float32
        ) + change.reshape(members, levels, width)
        return carry

    lax.fori_loop(0, points // width, step, 0, unroll=4)


def call(kernel, out, scratch, count, *operands):
    smem = pl.BlockSpec(memory_space=pltpu.SMEM)
    vmem = pl.BlockSpec(memory_space=pltpu.VMEM)
    return pl.pallas_call(
        kernel,
        out_shape=out,
        in_specs=[smem] * count + [vmem] * (len(operands) - count),
        out_specs=vmem,
        scratch_shapes=[scratch],
        compiler_params=pltpu.CompilerParams(vmem_limit_bytes=16 * 2**20),
    )(*operands)


def on_device(control, ensemble, vertical_loc, blocks, edge_mask, background, obs_precision):
    members, levels, points = control.shape
    tiles, slots, width, _ = blocks.shape
    rim = (slots - 1) // 2 * width
    ring, group = lax.axis_size("tile"), lax.axis_size("mem")
    even = 1 - lax.axis_index("tile") % 2
    even_ref = jnp.full((1,), even, jnp.int32)
    near = [(i, i ^ 1) for i in range(ring)]
    far = [(i, (i + 1 if i % 2 else i - 1) % ring) for i in range(ring)]

    def rims(value):
        axis = value.ndim - 1
        last = value.shape[axis] - rim
        to_near = lax.dynamic_slice_in_dim(value, even * last, rim, axis)
        to_far = lax.dynamic_slice_in_dim(value, (1 - even) * last, rim, axis)
        return lax.ppermute(to_near, "tile", near), lax.ppermute(to_far, "tile", far)

    control_near, control_far = rims(control)
    ensemble_near, ensemble_far = rims(ensemble)
    field = pltpu.VMEM((members * levels, points + 2 * rim), jnp.bfloat16)
    partial_sum = call(
        forward_kernel, jax.ShapeDtypeStruct((levels, points), jnp.bfloat16), field, 2,
        even_ref, edge_mask, vertical_loc, control, control_near, control_far, ensemble, blocks,
    )
    step = 1
    total = partial_sum
    while step < group:
        other = lax.ppermute(total, "mem", [(i, i ^ step) for i in range(group)])
        total = total.astype(jnp.float32) + other.astype(jnp.float32)
        step *= 2
        if step < group:
            total = total.astype(jnp.bfloat16)
    rows = levels // group
    increment = lax.dynamic_slice_in_dim(total, lax.axis_index("mem") * rows, rows, 0)
    depart = (obs_precision * (total - background)).astype(jnp.bfloat16)
    depart_near, depart_far = rims(depart)
    gradient = call(
        backward_kernel, jax.ShapeDtypeStruct((members, levels, points), jnp.float32), field, 2,
        even_ref, edge_mask, vertical_loc, control, depart, depart_near, depart_far, ensemble,
        ensemble_near, ensemble_far, blocks,
    )
    return increment, gradient


def solution(mesh):
    in_specs = (
        P("mem", None, "tile"),
        P("mem", None, "tile"),
        P(),
        P("tile", None, None, None),
        P("tile", None),
        P(None, "tile"),
        P(None, "tile"),
    )
    out_specs = (P("mem", "tile"), P("mem", None, "tile"))
    return jax.shard_map(
        on_device, mesh=mesh, in_specs=in_specs, out_specs=out_specs, check_vma=False
    )
```

```python
import jax
import jax.numpy as jnp
from jax import lax
from jax.experimental import pallas as pl
from jax.experimental.pallas import tpu as pltpu
from jax.sharding import PartitionSpec as P

CHUNK = 4


def slot_of(offset):
    return 2 * offset - 1 if offset > 0 else -2 * offset


def spread(loc, rows):
    levels = loc.shape[0]
    pick = (
        lax.broadcasted_iota(jnp.int32, (rows, levels), 0) % levels
        == lax.broadcasted_iota(jnp.int32, (rows, levels), 1)
    ).astype(jnp.bfloat16)
    tall = jnp.concatenate([loc] * (rows // levels), axis=0)
    wide = lax.dot_general(
        tall, pick, (((1,), (1,)), ((), ())), preferred_element_type=jnp.float32
    )
    same = (
        lax.broadcasted_iota(jnp.int32, (rows, rows), 0) // levels
        == lax.broadcasted_iota(jnp.int32, (rows, rows), 1) // levels
    )
    return jnp.where(same, wide, 0.0).astype(jnp.bfloat16)


def pair_rows(source, blocks_ref, pair):
    tiles, slots, width, _ = blocks_ref.shape
    reach = (slots - 1) // 2
    empty = jnp.zeros((width, width), jnp.bfloat16)
    lines = []
    for tile in range(2 * pair - reach, 2 * pair + reach + 2):
        line = []
        for row in (2 * pair, 2 * pair + 1):
            if abs(row - tile) > reach:
                line.append(empty)
            elif 0 <= tile < tiles:
                line.append(blocks_ref[tile, slot_of(row - tile)])
            else:
                line.append(blocks_ref[row, slot_of(tile - row)].T)
        lines.append(jnp.concatenate(line, axis=1))
    return jnp.dot(source, jnp.concatenate(lines, axis=0), preferred_element_type=jnp.float32)


def interior_pairs(tiles, reach):
    first = (reach + 1) // 2
    return range(first, tiles // 2 - first)


def edge_pairs(tiles, reach):
    first = (reach + 1) // 2
    return [*range(first), *range(tiles // 2 - first, tiles // 2)]


def edge_source(field_ref, rims_ref, pair, width, reach, tiles):
    low, high = 2 * pair - reach, 2 * pair + reach + 2
    rim = reach * width
    parts = []
    if low < 0:
        parts.append(rims_ref[:, rim + low * width : rim])
    parts.append(field_ref[:, max(low, 0) * width : min(high, tiles) * width])
    if high > tiles:
        parts.append(rims_ref[:, rim : rim + (high - tiles) * width])
    return jnp.concatenate(parts, axis=1)


def place_rims(rims_ref, even, near, far):
    rim = near.shape[1]
    rims_ref[:, pl.ds(pl.multiple_of(even * rim, rim), rim)] = near
    rims_ref[:, pl.ds(pl.multiple_of((1 - even) * rim, rim), rim)] = far


def contribution(ensemble_ref, rows, columns):
    members, levels, _ = ensemble_ref.shape
    weight = ensemble_ref[:, :, columns].astype(jnp.float32)
    return jnp.sum(weight * rows.reshape(members, levels, rows.shape[1]), axis=0).astype(
        jnp.bfloat16
    )


def take_rims(where_ref, control_hbm, ensemble_hbm, *refs):
    outs, sems = refs[:4], refs[4]
    rim = outs[0].shape[2]
    last = control_hbm.shape[2] - rim
    even = where_ref[0]
    starts = [pl.multiple_of(even * last, 128), pl.multiple_of((1 - even) * last, 128)] * 2
    copies = [
        pltpu.make_async_copy(source.at[:, :, pl.ds(start, rim)], out, sems.at[i])
        for i, (source, start, out) in enumerate(
            zip([control_hbm] * 2 + [ensemble_hbm] * 2, starts, outs)
        )
    ]
    for copy in copies:
        copy.start()
    for copy in copies:
        copy.wait()


def take_depart(where_ref, mine_ref, other_ref, background_ref, precision_ref, depart_ref,
                near_ref, far_ref, increment_ref):
    total = mine_ref[...].astype(jnp.float32) + other_ref[...].astype(jnp.float32)
    depart_ref[...] = (precision_ref[...] * (total - background_ref[...])).astype(jnp.bfloat16)
    even, place = where_ref[0], where_ref[1]
    rim = near_ref.shape[1]
    last = depart_ref.shape[1] - rim
    near_ref[...] = depart_ref[:, pl.ds(pl.multiple_of(even * last, 128), rim)]
    far_ref[...] = depart_ref[:, pl.ds(pl.multiple_of((1 - even) * last, 128), rim)]
    per = increment_ref.shape[0]
    rows = total[:per]
    for at in range(per, total.shape[0], per):
        rows = jnp.where(place == at // per, total[at : at + per], rows)
    increment_ref[...] = rows


def forward_interior(loc_ref, mask_hbm, control_hbm, ensemble_hbm, blocks_hbm, partial_ref,
                     field_ref, control_ref, ensemble_ref, blocks_ref, mask_ref, few_sems,
                     block_sems):
    members, levels, points = control_ref.shape
    tiles, slots, width, _ = blocks_ref.shape
    rows, reach = members * levels, (slots - 1) // 2
    chunks = [pl.ds(at, min(CHUNK, tiles - at)) for at in range(0, tiles, CHUNK)]
    block_copies = [
        pltpu.make_async_copy(blocks_hbm.at[at], blocks_ref.at[at], block_sems.at[i])
        for i, at in enumerate(chunks)
    ]
    control_copy = pltpu.make_async_copy(control_hbm, control_ref, few_sems.at[0])
    mask_copy = pltpu.make_async_copy(mask_hbm, mask_ref, few_sems.at[1])
    ensemble_copy = pltpu.make_async_copy(ensemble_hbm, ensemble_ref, few_sems.at[2])
    mask_copy.start()
    control_copy.start()
    block_copies[0].start()
    ensemble_copy.start()
    for copy in block_copies[1:]:
        copy.start()
    up = spread(loc_ref[...], rows)
    control_copy.wait()
    field_ref[...] = jnp.dot(
        up, control_ref[...].reshape(rows, points), preferred_element_type=jnp.float32
    ).astype(jnp.bfloat16)
    mask_copy.wait()
    ready = 0

    def take(until, ready):
        while ready < until:
            block_copies[ready].wait()
            at = chunks[ready].start
            for tile in range(at, at + chunks[ready].size):
                for slot in range(slots):
                    keep = mask_ref[slot, tile].astype(jnp.float32).astype(jnp.bfloat16)
                    blocks_ref[tile, slot] = blocks_ref[tile, slot] * keep
            ready += 1
        return ready

    for pair in interior_pairs(tiles, reach):
        high = 2 * pair + reach + 2
        ready = take(pl.cdiv(high, CHUNK), ready)
        if pair == interior_pairs(tiles, reach)[0]:
            ensemble_copy.wait()
        source = field_ref[:, (2 * pair - reach) * width : high * width]
        columns = slice(2 * pair * width, (2 * pair + 2) * width)
        partial_ref[:, columns] = contribution(
            ensemble_ref, pair_rows(source, blocks_ref, pair), columns
        )
    take(len(chunks), ready)


def forward_edge(where_ref, loc_ref, near_ref, far_ref, field_ref, ensemble_ref, blocks_ref,
                 interior_ref, partial_ref, rims_ref):
    members, levels, points = ensemble_ref.shape
    tiles, slots, width, _ = blocks_ref.shape
    rows, reach = members * levels, (slots - 1) // 2
    up = spread(loc_ref[...], rows)

    def vertical(ref):
        value = ref[...].reshape(rows, ref.shape[2])
        return jnp.dot(up, value, preferred_element_type=jnp.float32).astype(jnp.bfloat16)

    place_rims(rims_ref, where_ref[0], vertical(near_ref), vertical(far_ref))
    edges = edge_pairs(tiles, reach)
    inner = interior_pairs(tiles, reach)
    columns = slice(2 * inner[0] * width, 2 * (inner[-1] + 1) * width)
    partial_ref[:, columns] = interior_ref[:, columns]
    for pair in edges:
        source = edge_source(field_ref, rims_ref, pair, width, reach, tiles)
        columns = slice(2 * pair * width, (2 * pair + 2) * width)
        partial_ref[:, columns] = contribution(
            ensemble_ref, pair_rows(source, blocks_ref, pair), columns
        )


def weighted(value, depart):
    members, levels, points = value.shape
    product = value.astype(jnp.float32) * depart.astype(jnp.float32)[None]
    return product.astype(jnp.bfloat16).reshape(members * levels, points)


def write_rows(pairs, sources, control_ref, blocks_ref, gradient_hbm, stage_ref, sems):
    members, levels, _ = control_ref.shape
    width = blocks_ref.shape[2]
    copies = []
    for i, pair in enumerate(pairs):
        change = pair_rows(sources(pair), blocks_ref, pair)
        columns = pl.ds(2 * pair * width, 2 * width)
        staged = stage_ref.at[:, :, pl.ds(2 * i * width, 2 * width)]
        staged[...] = control_ref[:, :, columns].astype(jnp.float32) + change.reshape(
            members, levels, 2 * width
        )
        copy = pltpu.make_async_copy(staged, gradient_hbm.at[:, :, columns], sems.at[i])
        copy.start()
        copies.append(copy)
    for copy in copies:
        copy.wait()


def backward_interior(loc_ref, depart_ref, ensemble_ref, control_ref, blocks_ref, gradient_hbm,
                      field_ref, stage_ref, sems):
    members, levels, points = control_ref.shape
    tiles, slots, width, _ = blocks_ref.shape
    reach = (slots - 1) // 2
    down = spread(loc_ref[...].T, members * levels)
    field_ref[...] = jnp.dot(
        down, weighted(ensemble_ref[...], depart_ref[...]), preferred_element_type=jnp.float32
    ).astype(jnp.bfloat16)
    write_rows(
        interior_pairs(tiles, reach),
        lambda pair: field_ref[:, (2 * pair - reach) * width : (2 * pair + reach + 2) * width],
        control_ref, blocks_ref, gradient_hbm, stage_ref, sems,
    )


def backward_edge(where_ref, loc_ref, depart_near_ref, depart_far_ref, near_ref, far_ref,
                  field_ref, control_ref, blocks_ref, begun_hbm, gradient_hbm, rims_ref,
                  stage_ref, sems):
    members, levels, points = control_ref.shape
    tiles, slots, width, _ = blocks_ref.shape
    reach = (slots - 1) // 2
    down = spread(loc_ref[...].T, members * levels)

    def lowered(value_ref, depart_ref):
        return jnp.dot(
            down, weighted(value_ref[...], depart_ref[...]), preferred_element_type=jnp.float32
        ).astype(jnp.bfloat16)

    place_rims(
        rims_ref, where_ref[0], lowered(near_ref, depart_near_ref),
        lowered(far_ref, depart_far_ref),
    )
    write_rows(
        edge_pairs(tiles, reach),
        lambda pair: edge_source(field_ref, rims_ref, pair, width, reach, tiles),
        control_ref, blocks_ref, gradient_hbm, stage_ref, sems,
    )


SMEM = pl.BlockSpec(memory_space=pltpu.SMEM)
VMEM = pl.BlockSpec(memory_space=pltpu.VMEM)
HBM = pl.BlockSpec(memory_space=pltpu.HBM)


def call(kernel, outs, out_specs, in_specs, scratch, mib, cost, *operands, aliases=None):
    return pl.pallas_call(
        kernel,
        out_shape=outs,
        in_specs=in_specs,
        out_specs=out_specs,
        scratch_shapes=scratch,
        input_output_aliases=aliases or {},
        cost_estimate=pl.CostEstimate(flops=cost[0], bytes_accessed=cost[1], transcendentals=0),
        compiler_params=pltpu.CompilerParams(vmem_limit_bytes=mib * 2**20),
    )(*operands)


def on_device(control, ensemble, vertical_loc, blocks, edge_mask, background, obs_precision):
    members, levels, points = control.shape
    tiles, slots, width, _ = blocks.shape
    reach = (slots - 1) // 2
    rim, rows = reach * width, members * levels
    ring, group = lax.axis_size("tile"), lax.axis_size("mem")
    per = levels // group
    where_ref = jnp.stack([1 - lax.axis_index("tile") % 2, lax.axis_index("mem")])
    near = [(i, i ^ 1) for i in range(ring)]
    far = [(i, (i + 1 if i % 2 else i - 1) % ring) for i in range(ring)]

    def exchange(to_near, to_far):
        return lax.ppermute(to_near, "tile", near), lax.ppermute(to_far, "tile", far)

    def shape(dims, dtype):
        return jax.ShapeDtypeStruct(dims, dtype)

    def in_hbm(value):
        return pltpu.with_memory_space_constraint(value, pltpu.HBM)

    dma = pltpu.SemaphoreType.DMA
    inner, outer = len(interior_pairs(tiles, reach)), len(edge_pairs(tiles, reach))
    pair_flops = 2 * rows * (2 * reach + 2) * width * 2 * width
    rim_shape = shape((members, levels, rim), jnp.bfloat16)
    sends = call(
        take_rims, [rim_shape] * 4, [VMEM] * 4, [SMEM, HBM, HBM], [dma((4,))], 2,
        (0, 16 * rows * rim), where_ref, in_hbm(control), in_hbm(ensemble),
    )
    control_near, control_far = exchange(*sends[:2])
    ensemble_near, ensemble_far = exchange(*sends[2:])
    inside, field, control, ensemble, blocks = call(
        forward_interior,
        [
            shape((levels, points), jnp.bfloat16),
            shape((rows, points), jnp.bfloat16),
            shape(control.shape, control.dtype),
            shape(ensemble.shape, ensemble.dtype),
            shape(blocks.shape, blocks.dtype),
        ],
        [VMEM] * 5,
        [VMEM, HBM, HBM, HBM, HBM],
        [pltpu.SMEM((slots, tiles), edge_mask.dtype), dma((3,)), dma((pl.cdiv(tiles, CHUNK),))],
        16,
        (inner * pair_flops, blocks.size * 2 + 4 * control.size),
        vertical_loc, *(in_hbm(v) for v in (edge_mask.T, control, ensemble, blocks)),
    )
    partial_sum = call(
        forward_edge,
        shape((levels, points), jnp.bfloat16),
        VMEM,
        [SMEM] + [VMEM] * 7,
        [pltpu.VMEM((rows, 2 * rim), jnp.bfloat16)],
        4,
        (outer * pair_flops, 4 * rows * rim),
        where_ref, vertical_loc, control_near, control_far, field, ensemble, blocks, inside,
    )
    step = 1
    total = partial_sum
    while True:
        other = lax.ppermute(total, "mem", [(i, i ^ step) for i in range(group)])
        step *= 2
        if step >= group:
            break
        total = (total.astype(jnp.float32) + other.astype(jnp.float32)).astype(jnp.bfloat16)
    depart_rim = shape((levels, rim), jnp.bfloat16)
    depart, to_near, to_far, increment = call(
        take_depart,
        [
            shape((levels, points), jnp.bfloat16), depart_rim, depart_rim,
            shape((per, points), jnp.float32),
        ],
        [VMEM] * 4,
        [SMEM] + [VMEM] * 4,
        [],
        4,
        (4 * levels * points, 16 * levels * points),
        where_ref, total, other, background, obs_precision,
    )
    depart_near, depart_far = exchange(to_near, to_far)
    full = shape((members, levels, points), jnp.float32)
    gradient, field = call(
        backward_interior,
        [full, shape((rows, points), jnp.bfloat16)],
        [HBM, VMEM],
        [VMEM] * 5,
        [pltpu.VMEM((members, levels, 2 * inner * width), jnp.float32), dma((inner,))],
        8,
        (inner * pair_flops, 4 * control.size),
        vertical_loc, depart, ensemble, control, blocks,
    )
    gradient = call(
        backward_edge,
        full,
        HBM,
        [SMEM] + [VMEM] * 8 + [HBM],
        [
            pltpu.VMEM((rows, 2 * rim), jnp.bfloat16),
            pltpu.VMEM((members, levels, 2 * outer * width), jnp.float32),
            dma((outer,)),
        ],
        4,
        (outer * pair_flops, 4 * rows * rim),
        where_ref, vertical_loc, depart_near, depart_far, ensemble_near, ensemble_far, field,
        control, blocks, gradient,
        aliases={9: 0},
    )
    return increment, gradient


def solution(mesh):
    in_specs = (
        P("mem", None, "tile"),
        P("mem", None, "tile"),
        P(),
        P("tile", None, None, None),
        P("tile", None),
        P(None, "tile"),
        P(None, "tile"),
    )
    out_specs = (P("mem", "tile"), P("mem", None, "tile"))
    return jax.shard_map(
        on_device, mesh=mesh, in_specs=in_specs, out_specs=out_specs, check_vma=False
    )
```

```python
import jax
import jax.numpy as jnp
from jax import lax
from jax.experimental import pallas as pl
from jax.experimental.pallas import tpu as pltpu
from jax.sharding import PartitionSpec as P

LOADED = 60 * 2**20
LANES = 128


def slot_of(offset):
    return 2 * offset - 1 if offset > 0 else -2 * offset


def even_tile():
    return 1 - lax.rem(lax.axis_index("tile"), 2)


def spread(loc, rows):
    levels = loc.shape[0]
    pick = (
        lax.broadcasted_iota(jnp.int32, (rows, levels), 0) % levels
        == lax.broadcasted_iota(jnp.int32, (rows, levels), 1)
    ).astype(jnp.bfloat16)
    tall = jnp.concatenate([loc] * (rows // levels), axis=0)
    wide = lax.dot_general(
        tall, pick, (((1,), (1,)), ((), ())), preferred_element_type=jnp.float32
    )
    same = (
        lax.broadcasted_iota(jnp.int32, (rows, rows), 0) // levels
        == lax.broadcasted_iota(jnp.int32, (rows, rows), 1) // levels
    )
    return jnp.where(same, wide, 0.0).astype(jnp.bfloat16)


def pair_rows(field_ref, block_at, shape, pair):
    tiles, slots, width, _ = shape
    reach = (slots - 1) // 2
    empty = jnp.zeros((width, width), jnp.bfloat16)
    low, high = max(2 * pair - reach, 0), min(2 * pair + reach + 2, tiles)
    lines = []
    for tile in range(low, high):
        line = [
            block_at(tile, slot_of(row - tile)) if abs(row - tile) <= reach else empty
            for row in (2 * pair, 2 * pair + 1)
        ]
        lines.append(jnp.concatenate(line, axis=1))
    source = field_ref[:, low * width : high * width]
    return jnp.dot(source, jnp.concatenate(lines, axis=0), preferred_element_type=jnp.float32)


def contribution(weight, rows):
    members, levels, columns = weight.shape
    return jnp.sum(weight.astype(jnp.float32) * rows.reshape(members, levels, columns), axis=0)


def take_rims(control_hbm, far_ref, near_ref, sems):
    rim = near_ref.shape[2]
    last = control_hbm.shape[2] - rim
    even = even_tile()
    copies = [
        pltpu.make_async_copy(
            control_hbm.at[:, :, pl.ds(pl.multiple_of(side * last, LANES), rim)], ref, sems.at[i]
        )
        for i, (side, ref) in enumerate(((even, near_ref), (1 - even, far_ref)))
    ]
    for copy in copies:
        copy.start()
    for copy in copies:
        copy.wait()


def pass_on(far_ref, near_ref, far_out, near_out):
    pass


def forward_local(loc_ref, mask_hbm, control_ref, ensemble_ref, raw_ref, partial_ref, blocks_ref,
                  up_ref, down_ref, edge_ref, far_ref, near_ref, field_ref, mask_ref, sem):
    members, levels, points = control_ref.shape
    tiles, slots, width, _ = blocks_ref.shape
    rows, reach = members * levels, (slots - 1) // 2
    rim = reach * width
    mask_copy = pltpu.make_async_copy(mask_hbm, mask_ref, sem)
    mask_copy.start()
    up = spread(loc_ref[...], rows)
    up_ref[...] = up
    down_ref[...] = up.T
    field_ref[...] = jnp.dot(
        up, control_ref[...].reshape(rows, points), preferred_element_type=jnp.float32
    ).astype(jnp.bfloat16)
    even = even_tile()
    for side, ref in ((even, near_ref), (1 - even, far_ref)):
        at = pl.multiple_of(side * (points - rim), LANES)
        ref[...] = ensemble_ref[:, :, pl.ds(at, rim)]
    mask_copy.wait()

    def masked(tile, slot):
        keep = mask_ref[slot, tile].astype(jnp.float32).astype(jnp.bfloat16)
        return raw_ref[tile, slot] * keep

    def kept(tile, slot):
        block = masked(tile, slot)
        blocks_ref[tile, slot] = block
        return block

    for pair in range(tiles // 2):
        columns = slice(2 * pair * width, (2 * pair + 2) * width)
        partial_ref[:, columns] = contribution(
            ensemble_ref[:, :, columns], pair_rows(field_ref, kept, raw_ref.shape, pair)
        )
    empty = jnp.zeros((width, width), jnp.bfloat16)
    for side, first, source in ((0, 0, -reach), (1, tiles - reach, tiles)):
        for i in range(reach):
            for j in range(reach):
                offset = source + i - first - j
                block = empty
                if abs(offset) <= reach:
                    block = masked(first + j, slot_of(offset)).T
                edge_ref[side, i * width : (i + 1) * width, j * width : (j + 1) * width] = block


def forward_edge(near_ref, far_ref, up_ref, edge_ref, ensemble_ref, local_ref, partial_ref):
    members, levels, points = ensemble_ref.shape
    rows, rim = members * levels, near_ref.shape[2]
    partial_ref[...] = local_ref[...].astype(jnp.bfloat16)
    even = even_tile()
    for side, ref in ((even, near_ref), (1 - even, far_ref)):
        at = pl.multiple_of(side * (points - rim), LANES)
        vertical = jnp.dot(
            up_ref[...], ref[...].reshape(rows, rim), preferred_element_type=jnp.float32
        ).astype(jnp.bfloat16)
        change = jnp.dot(vertical, edge_ref[side], preferred_element_type=jnp.float32)
        columns = pl.ds(at, rim)
        partial_ref[:, columns] = (
            local_ref[:, columns] + contribution(ensemble_ref[:, :, columns], change)
        ).astype(jnp.bfloat16)


def take_depart(mine_ref, other_ref, background_ref, precision_ref, far_ref, near_ref, depart_ref,
                total_ref):
    total = mine_ref[...].astype(jnp.float32) + other_ref[...].astype(jnp.float32)
    total_ref[...] = total
    depart_ref[...] = (precision_ref[...] * (total - background_ref[...])).astype(jnp.bfloat16)
    rim = near_ref.shape[1]
    even = even_tile()
    for side, ref in ((even, near_ref), (1 - even, far_ref)):
        at = pl.multiple_of(side * (depart_ref.shape[1] - rim), LANES)
        ref[...] = depart_ref[:, pl.ds(at, rim)]


def weighted(value, depart):
    members, levels, points = value.shape
    product = value.astype(jnp.float32) * depart.astype(jnp.float32)[None]
    return product.astype(jnp.bfloat16).reshape(members * levels, points)


def backward_local(depart_ref, total_ref, ensemble_ref, control_ref, blocks_ref, down_ref,
                   gradient_hbm, edge_ref, increment_ref, field_ref, stage_ref, sems):
    members, levels, points = control_ref.shape
    tiles, slots, width, _ = blocks_ref.shape
    reach = (slots - 1) // 2
    field_ref[...] = jnp.dot(
        down_ref[...], weighted(ensemble_ref[...], depart_ref[...]),
        preferred_element_type=jnp.float32,
    ).astype(jnp.bfloat16)
    copies = []

    def block_at(tile, slot):
        return blocks_ref[tile, slot]

    for pair in range(tiles // 2):
        at = 2 * pair * width
        change = pair_rows(field_ref, block_at, blocks_ref.shape, pair).reshape(members, levels, 2 * width)
        control = control_ref[:, :, at : at + 2 * width].astype(jnp.float32)
        stage_ref[:, :, at : at + 2 * width] = control + change
        first, last = max(2 * pair, reach), min(2 * pair + 2, tiles - reach)
        if first < last:
            columns = pl.ds(first * width, (last - first) * width)
            copy = pltpu.make_async_copy(
                stage_ref.at[:, :, columns], gradient_hbm.at[:, :, columns], sems.at[pair]
            )
            copy.start()
            copies.append(copy)
    rim = reach * width
    edge_ref[0] = stage_ref[:, :, :rim]
    edge_ref[1] = stage_ref[:, :, points - rim :]
    place, per = lax.axis_index("mem"), increment_ref.shape[0]
    rows = total_ref[:per]
    for at in range(per, levels, per):
        rows = jnp.where(place == at // per, total_ref[at : at + per], rows)
    increment_ref[...] = rows
    for copy in copies:
        copy.wait()


def backward_edge(depart_near_ref, depart_far_ref, near_ref, far_ref, down_ref, edge_ref,
                  begun_ref, begun_hbm, gradient_hbm, stage_ref, sems):
    members, levels, rim = near_ref.shape
    points = gradient_hbm.shape[2]
    even = even_tile()
    copies = []
    for i, (side, value_ref, depart_ref) in enumerate(
        ((even, near_ref, depart_near_ref), (1 - even, far_ref, depart_far_ref))
    ):
        lowered = jnp.dot(
            down_ref[...], weighted(value_ref[...], depart_ref[...]),
            preferred_element_type=jnp.float32,
        ).astype(jnp.bfloat16)
        change = jnp.dot(lowered, edge_ref[side], preferred_element_type=jnp.float32)
        stage_ref[i] = begun_ref[side] + change.reshape(members, levels, rim)
        at = pl.multiple_of(side * (points - rim), LANES)
        copy = pltpu.make_async_copy(
            stage_ref.at[i], gradient_hbm.at[:, :, pl.ds(at, rim)], sems.at[i]
        )
        copy.start()
        copies.append(copy)
    for copy in copies:
        copy.wait()


VMEM = pl.BlockSpec(memory_space=pltpu.VMEM)
HBM = pl.BlockSpec(memory_space=pltpu.HBM)


def call(kernel, outs, out_specs, in_specs, scratch, mib, cost, *operands, aliases=None):
    return pl.pallas_call(
        kernel,
        out_shape=outs,
        in_specs=in_specs,
        out_specs=out_specs,
        scratch_shapes=scratch,
        input_output_aliases=aliases or {},
        cost_estimate=pl.CostEstimate(flops=cost[0], bytes_accessed=cost[1], transcendentals=0),
        compiler_params=pltpu.CompilerParams(vmem_limit_bytes=mib * 2**20),
    )(*operands)


def on_device(control, ensemble, vertical_loc, blocks, edge_mask, background, obs_precision):
    members, levels, points = control.shape
    tiles, slots, width, _ = blocks.shape
    reach = (slots - 1) // 2
    rim, rows = reach * width, members * levels
    ring, group = lax.axis_size("tile"), lax.axis_size("mem")
    per = levels // group
    near = [(i, i ^ 1) for i in range(ring)]
    far = [(i, (i + 1 if i % 2 else i - 1) % ring) for i in range(ring)]

    def exchange(to_far, to_near):
        from_far = lax.ppermute(to_far, "tile", far)
        return lax.ppermute(to_near, "tile", near), from_far

    def half(*dims):
        return jax.ShapeDtypeStruct(dims, jnp.bfloat16)

    def single(*dims):
        return jax.ShapeDtypeStruct(dims, jnp.float32)

    def in_hbm(value):
        return pltpu.with_memory_space_constraint(value, pltpu.HBM)

    dma = pltpu.SemaphoreType.DMA
    local_flops = 2 * rows * (tiles // 2) * (2 * reach + 2) * width * 2 * width
    edge_flops = 4 * rows * rim * (rows + rim)
    sends = call(
        take_rims, [half(members, levels, rim)] * 2, [VMEM] * 2, [HBM], [dma((2,))], 2,
        (0, 8 * rows * rim), in_hbm(control),
    )
    sends = call(
        pass_on, [half(members, levels, rim)] * 2, [VMEM] * 2, [VMEM] * 2, [], 2,
        (LOADED * 10**6, LOADED * 1000), *sends, aliases={0: 0, 1: 1},
    )
    control_near, control_far = exchange(*sends)
    partial_sum, masked, up, down, edge, to_far, to_near = call(
        forward_local,
        [
            single(levels, points), half(*blocks.shape), half(rows, rows), half(rows, rows),
            half(2, rim, rim), half(members, levels, rim), half(members, levels, rim),
        ],
        [VMEM] * 7,
        [VMEM, HBM, VMEM, VMEM, VMEM],
        [
            pltpu.VMEM((rows, points), jnp.bfloat16),
            pltpu.SMEM((slots, tiles), edge_mask.dtype), dma,
        ],
        16,
        (local_flops, blocks.size * 2 + 4 * control.size),
        vertical_loc, in_hbm(edge_mask.T), control, ensemble, blocks,
    )
    ensemble_near, ensemble_far = exchange(to_far, to_near)
    total = call(
        forward_edge, half(levels, points), VMEM, [VMEM] * 6, [], 4,
        (edge_flops, 4 * rows * rim),
        control_near, control_far, up, edge, ensemble, partial_sum,
    )
    step = 1
    while True:
        other = lax.ppermute(total, "mem", [(i, i ^ step) for i in range(group)])
        step *= 2
        if step >= group:
            break
        total = (total.astype(jnp.float32) + other.astype(jnp.float32)).astype(jnp.bfloat16)
    to_far, to_near, depart, total = call(
        take_depart,
        [half(levels, rim), half(levels, rim), half(levels, points), single(levels, points)],
        [VMEM] * 4, [VMEM] * 4, [], 4,
        (4 * levels * points, 16 * levels * points),
        total, other, background, obs_precision,
    )
    depart_near, depart_far = exchange(to_far, to_near)
    full = single(members, levels, points)
    gradient, begun, increment = call(
        backward_local,
        [full, single(2, members, levels, rim), single(per, points)],
        [HBM, VMEM, VMEM],
        [VMEM] * 6,
        [
            pltpu.VMEM((rows, points), jnp.bfloat16),
            pltpu.VMEM((members, levels, points), jnp.float32), dma((tiles // 2,)),
        ],
        8,
        (local_flops, 4 * control.size),
        depart, total, ensemble, control, masked, down,
    )
    gradient = call(
        backward_edge, full, HBM, [VMEM] * 7 + [HBM],
        [pltpu.VMEM((2, members, levels, rim), jnp.float32), dma((2,))],
        4,
        (edge_flops, 4 * rows * rim),
        depart_near, depart_far, ensemble_near, ensemble_far, down, edge, begun, gradient,
        aliases={7: 0},
    )
    return increment, gradient


def solution(mesh):
    in_specs = (
        P("mem", None, "tile"),
        P("mem", None, "tile"),
        P(),
        P("tile", None, None, None),
        P("tile", None),
        P(None, "tile"),
        P(None, "tile"),
    )
    out_specs = (P("mem", "tile"), P("mem", None, "tile"))
    return jax.shard_map(
        on_device, mesh=mesh, in_specs=in_specs, out_specs=out_specs, check_vma=False
    )
```

```python
import jax
import jax.numpy as jnp
from jax import lax
from jax.experimental import pallas as pl
from jax.experimental.pallas import tpu as pltpu
from jax.sharding import PartitionSpec as P

LOADED = 60 * 2**20
LANES = 128


def slot_of(offset):
    return 2 * offset - 1 if offset > 0 else -2 * offset


def even_tile():
    return 1 - lax.rem(lax.axis_index("tile"), 2)


def spread(loc, rows):
    levels = loc.shape[0]
    pick = (
        lax.broadcasted_iota(jnp.int32, (rows, levels), 0) % levels
        == lax.broadcasted_iota(jnp.int32, (rows, levels), 1)
    ).astype(jnp.bfloat16)
    tall = jnp.concatenate([loc] * (rows // levels), axis=0)
    wide = lax.dot_general(
        tall, pick, (((1,), (1,)), ((), ())), preferred_element_type=jnp.float32
    )
    same = (
        lax.broadcasted_iota(jnp.int32, (rows, rows), 0) // levels
        == lax.broadcasted_iota(jnp.int32, (rows, rows), 1) // levels
    )
    return jnp.where(same, wide, 0.0).astype(jnp.bfloat16)


def pair_rows(field_ref, block_at, shape, pair):
    tiles, slots, width, _ = shape
    reach = (slots - 1) // 2
    empty = jnp.zeros((width, width), jnp.bfloat16)
    low, high = max(2 * pair - reach, 0), min(2 * pair + reach + 2, tiles)
    lines = []
    for tile in range(low, high):
        line = [
            block_at(tile, slot_of(row - tile)) if abs(row - tile) <= reach else empty
            for row in (2 * pair, 2 * pair + 1)
        ]
        lines.append(jnp.concatenate(line, axis=1))
    source = field_ref[:, low * width : high * width]
    return jnp.dot(source, jnp.concatenate(lines, axis=0), preferred_element_type=jnp.float32)


def contribution(weight, rows):
    members, levels, columns = weight.shape
    return jnp.sum(weight.astype(jnp.float32) * rows.reshape(members, levels, columns), axis=0)


def take_rims(control_hbm, last_ref, first_ref, sems):
    rim = last_ref.shape[2]
    points = control_hbm.shape[2]
    copies = [
        pltpu.make_async_copy(control_hbm.at[:, :, pl.ds(at, rim)], ref, sems.at[i])
        for i, (at, ref) in enumerate(((points - rim, last_ref), (0, first_ref)))
    ]
    for copy in copies:
        copy.start()
    for copy in copies:
        copy.wait()


def pass_on(last_ref, first_ref, last_out, first_out):
    pass


def forward_local(loc_ref, mask_hbm, control_ref, ensemble_ref, raw_ref, inner_ref, outer_ref,
                  blocks_ref, up_ref, down_ref, edge_ref, far_ref, field_ref, mask_ref, sem):
    members, levels, points = control_ref.shape
    tiles, slots, width, _ = blocks_ref.shape
    rows, reach = members * levels, (slots - 1) // 2
    rim = reach * width
    mask_copy = pltpu.make_async_copy(mask_hbm, mask_ref, sem)
    mask_copy.start()
    up = spread(loc_ref[...], rows)
    up_ref[...] = up
    down_ref[...] = up.T
    field_ref[...] = jnp.dot(
        up, control_ref[...].reshape(rows, points), preferred_element_type=jnp.float32
    ).astype(jnp.bfloat16)
    at = pl.multiple_of((1 - even_tile()) * (points - rim), LANES)
    far_ref[...] = ensemble_ref[:, :, pl.ds(at, rim)]
    mask_copy.wait()

    def masked(tile, slot):
        keep = mask_ref[slot, tile].astype(jnp.float32).astype(jnp.bfloat16)
        return raw_ref[tile, slot] * keep

    def kept(tile, slot):
        block = masked(tile, slot)
        blocks_ref[tile, slot] = block
        return block

    for pair in range(tiles // 2):
        columns = slice(2 * pair * width, (2 * pair + 2) * width)
        part = contribution(
            ensemble_ref[:, :, columns], pair_rows(field_ref, kept, raw_ref.shape, pair)
        )
        for i, tile in enumerate((2 * pair, 2 * pair + 1)):
            value = part[:, i * width : (i + 1) * width]
            if reach <= tile < tiles - reach:
                at = (tile - reach) * width
                inner_ref[:, at : at + width] = value.astype(jnp.bfloat16)
            else:
                at = (tile if tile < reach else tile - tiles + 2 * reach) * width
                outer_ref[:, at : at + width] = value
    empty = jnp.zeros((width, width), jnp.bfloat16)
    for side, first, source in ((0, 0, -reach), (1, tiles - reach, tiles)):
        for i in range(reach):
            for j in range(reach):
                offset = source + i - first - j
                block = empty
                if abs(offset) <= reach:
                    block = masked(first + j, slot_of(offset)).T
                edge_ref[side, i * width : (i + 1) * width, j * width : (j + 1) * width] = block


def forward_edge(left_ref, right_ref, up_ref, edge_ref, ensemble_ref, outer_ref, partial_ref):
    members, levels, points = ensemble_ref.shape
    rows, rim = members * levels, left_ref.shape[2]
    for side, ref in ((0, left_ref), (1, right_ref)):
        vertical = jnp.dot(
            up_ref[...], ref[...].reshape(rows, rim), preferred_element_type=jnp.float32
        ).astype(jnp.bfloat16)
        change = jnp.dot(vertical, edge_ref[side], preferred_element_type=jnp.float32)
        at, columns = side * (points - rim), slice(side * rim, (side + 1) * rim)
        added = contribution(ensemble_ref[:, :, at : at + rim], change)
        partial_ref[:, columns] = (outer_ref[:, columns] + added).astype(jnp.bfloat16)


def weighted(value, depart):
    members, levels, points = value.shape
    product = value.astype(jnp.float32) * depart.astype(jnp.float32)[None]
    return product.astype(jnp.bfloat16).reshape(members * levels, points)


def take_depart(inner_ref, inner_other_ref, outer_ref, outer_other_ref, background_ref,
                precision_ref, ensemble_ref, near_ref, far_ref, depart_ref, total_ref):
    rim = far_ref.shape[1]
    points = depart_ref.shape[1]
    inner = inner_ref[...].astype(jnp.float32) + inner_other_ref[...].astype(jnp.float32)
    outer = outer_ref[...].astype(jnp.float32) + outer_other_ref[...].astype(jnp.float32)
    total_ref[:, :rim] = outer[:, :rim]
    total_ref[:, rim : points - rim] = inner
    total_ref[:, points - rim :] = outer[:, rim:]
    depart_ref[...] = (precision_ref[...] * (total_ref[...] - background_ref[...])).astype(
        jnp.bfloat16
    )
    even = even_tile()
    near = pl.ds(pl.multiple_of(even * (points - rim), LANES), rim)
    far = pl.ds(pl.multiple_of((1 - even) * (points - rim), LANES), rim)
    near_ref[...] = weighted(ensemble_ref[:, :, near], depart_ref[:, near])
    far_ref[...] = depart_ref[:, far]


def backward_local(depart_ref, total_ref, ensemble_ref, control_ref, blocks_ref, down_ref,
                   gradient_hbm, edge_ref, increment_ref, field_ref, stage_ref, sems):
    members, levels, points = control_ref.shape
    tiles, slots, width, _ = blocks_ref.shape
    reach = (slots - 1) // 2
    field_ref[...] = jnp.dot(
        down_ref[...], weighted(ensemble_ref[...], depart_ref[...]),
        preferred_element_type=jnp.float32,
    ).astype(jnp.bfloat16)
    copies = []

    def block_at(tile, slot):
        return blocks_ref[tile, slot]

    for pair in range(tiles // 2):
        at = 2 * pair * width
        change = pair_rows(field_ref, block_at, blocks_ref.shape, pair).reshape(members, levels, 2 * width)
        control = control_ref[:, :, at : at + 2 * width].astype(jnp.float32)
        stage_ref[:, :, at : at + 2 * width] = control + change
        first, last = max(2 * pair, reach), min(2 * pair + 2, tiles - reach)
        if first < last:
            columns = pl.ds(first * width, (last - first) * width)
            copy = pltpu.make_async_copy(
                stage_ref.at[:, :, columns], gradient_hbm.at[:, :, columns], sems.at[pair]
            )
            copy.start()
            copies.append(copy)
    rim = reach * width
    edge_ref[0] = stage_ref[:, :, :rim]
    edge_ref[1] = stage_ref[:, :, points - rim :]
    place, per = lax.axis_index("mem"), increment_ref.shape[0]
    rows = total_ref[:per]
    for at in range(per, levels, per):
        rows = jnp.where(place == at // per, total_ref[at : at + per], rows)
    increment_ref[...] = rows
    for copy in copies:
        copy.wait()


def backward_edge(near_ref, depart_ref, far_ref, down_ref, edge_ref, begun_ref, begun_hbm,
                  gradient_hbm, stage_ref, sems):
    members, levels, rim = far_ref.shape
    points = gradient_hbm.shape[2]
    even = even_tile()
    copies = []
    for i, (side, value) in enumerate(
        ((even, near_ref[...]), (1 - even, weighted(far_ref[...], depart_ref[...])))
    ):
        lowered = jnp.dot(down_ref[...], value, preferred_element_type=jnp.float32)
        change = jnp.dot(
            lowered.astype(jnp.bfloat16), edge_ref[side], preferred_element_type=jnp.float32
        )
        stage_ref[i] = begun_ref[side] + change.reshape(members, levels, rim)
        at = pl.multiple_of(side * (points - rim), LANES)
        copy = pltpu.make_async_copy(
            stage_ref.at[i], gradient_hbm.at[:, :, pl.ds(at, rim)], sems.at[i]
        )
        copy.start()
        copies.append(copy)
    for copy in copies:
        copy.wait()


VMEM = pl.BlockSpec(memory_space=pltpu.VMEM)
HBM = pl.BlockSpec(memory_space=pltpu.HBM)


def call(kernel, outs, out_specs, in_specs, scratch, mib, cost, *operands, aliases=None):
    return pl.pallas_call(
        kernel,
        out_shape=outs,
        in_specs=in_specs,
        out_specs=out_specs,
        scratch_shapes=scratch,
        input_output_aliases=aliases or {},
        cost_estimate=pl.CostEstimate(flops=cost[0], bytes_accessed=cost[1], transcendentals=0),
        compiler_params=pltpu.CompilerParams(vmem_limit_bytes=mib * 2**20),
    )(*operands)


def on_device(control, ensemble, vertical_loc, blocks, edge_mask, background, obs_precision):
    members, levels, points = control.shape
    tiles, slots, width, _ = blocks.shape
    reach = (slots - 1) // 2
    rim, rows = reach * width, members * levels
    ring, group = lax.axis_size("tile"), lax.axis_size("mem")
    per = levels // group
    after = [(i, (i + 1) % ring) for i in range(ring)]
    before = [(j, i) for i, j in after]

    near = [(i, i ^ 1) for i in range(ring)]
    far = [(i, (i + 1 if i % 2 else i - 1) % ring) for i in range(ring)]

    def half(*dims):
        return jax.ShapeDtypeStruct(dims, jnp.bfloat16)

    def single(*dims):
        return jax.ShapeDtypeStruct(dims, jnp.float32)

    def in_hbm(value):
        return pltpu.with_memory_space_constraint(value, pltpu.HBM)

    dma = pltpu.SemaphoreType.DMA
    local_flops = 2 * rows * (tiles // 2) * (2 * reach + 2) * width * 2 * width
    edge_flops = 4 * rows * rim * (rows + rim)
    sends = call(
        take_rims, [half(members, levels, rim)] * 2, [VMEM] * 2, [HBM], [dma((2,))], 2,
        (0, 8 * rows * rim), in_hbm(control),
    )
    sends = call(
        pass_on, [half(members, levels, rim)] * 2, [VMEM] * 2, [VMEM] * 2, [], 2,
        (LOADED * 10**6, LOADED * 1000), *sends, aliases={0: 0, 1: 1},
    )
    control_left = lax.ppermute(sends[0], "tile", after)
    control_right = lax.ppermute(sends[1], "tile", before)
    inner, outer, masked, up, down, edge, to_far = call(
        forward_local,
        [
            half(levels, points - 2 * rim), single(levels, 2 * rim), half(*blocks.shape), half(rows, rows), half(rows, rows),
            half(2, rim, rim), half(members, levels, rim),
        ],
        [VMEM] * 7,
        [VMEM, HBM, VMEM, VMEM, VMEM],
        [
            pltpu.VMEM((rows, points), jnp.bfloat16),
            pltpu.SMEM((slots, tiles), edge_mask.dtype), dma,
        ],
        16,
        (local_flops, blocks.size * 2 + 4 * control.size),
        vertical_loc, in_hbm(edge_mask.T), control, ensemble, blocks,
    )
    ensemble_far = lax.ppermute(to_far, "tile", far)
    outer = call(
        forward_edge, half(levels, 2 * rim), VMEM, [VMEM] * 6, [], 4,
        (edge_flops, 4 * rows * rim),
        control_left, control_right, up, edge, ensemble, outer,
    )

    def other_half(value, step):
        return lax.ppermute(value, "mem", [(i, i ^ step) for i in range(group)])

    step = 1
    while 2 * step < group:
        inner, outer = [
            (value.astype(jnp.float32) + other_half(value, step).astype(jnp.float32)).astype(
                jnp.bfloat16
            )
            for value in (inner, outer)
        ]
        step *= 2
    to_near, to_far, depart, total = call(
        take_depart,
        [half(rows, rim), half(levels, rim), half(levels, points), single(levels, points)],
        [VMEM] * 4, [VMEM] * 7, [], 4,
        (4 * levels * points, 16 * levels * points),
        inner, other_half(inner, step), outer, other_half(outer, step), background, obs_precision,
        ensemble,
    )
    weighted_near = lax.ppermute(to_near, "tile", near)
    depart_far = lax.ppermute(to_far, "tile", far)
    full = single(members, levels, points)
    gradient, begun, increment = call(
        backward_local,
        [full, single(2, members, levels, rim), single(per, points)],
        [HBM, VMEM, VMEM],
        [VMEM] * 6,
        [
            pltpu.VMEM((rows, points), jnp.bfloat16),
            pltpu.VMEM((members, levels, points), jnp.float32), dma((tiles // 2,)),
        ],
        8,
        (local_flops, 4 * control.size),
        depart, total, ensemble, control, masked, down,
    )
    gradient = call(
        backward_edge, full, HBM, [VMEM] * 6 + [HBM],
        [pltpu.VMEM((2, members, levels, rim), jnp.float32), dma((2,))],
        4,
        (edge_flops, 4 * rows * rim),
        weighted_near, depart_far, ensemble_far, down, edge, begun, gradient,
        aliases={6: 0},
    )
    return increment, gradient


def solution(mesh):
    in_specs = (
        P("mem", None, "tile"),
        P("mem", None, "tile"),
        P(),
        P("tile", None, None, None),
        P("tile", None),
        P(None, "tile"),
        P(None, "tile"),
    )
    out_specs = (P("mem", "tile"), P("mem", None, "tile"))
    return jax.shard_map(
        on_device, mesh=mesh, in_specs=in_specs, out_specs=out_specs, check_vma=False
    )
```

```python
import jax
import jax.numpy as jnp
from jax import lax
from jax.experimental import pallas as pl
from jax.experimental.pallas import tpu as pltpu
from jax.sharding import PartitionSpec as P

LOADED = 60 * 2**20


def slot_of(offset):
    return 2 * offset - 1 if offset > 0 else -2 * offset


def spread(loc, rows):
    levels = loc.shape[0]
    pick = (
        lax.broadcasted_iota(jnp.int32, (rows, levels), 0) % levels
        == lax.broadcasted_iota(jnp.int32, (rows, levels), 1)
    ).astype(jnp.bfloat16)
    tall = jnp.concatenate([loc] * (rows // levels), axis=0)
    wide = lax.dot_general(
        tall, pick, (((1,), (1,)), ((), ())), preferred_element_type=jnp.float32
    )
    same = (
        lax.broadcasted_iota(jnp.int32, (rows, rows), 0) // levels
        == lax.broadcasted_iota(jnp.int32, (rows, rows), 1) // levels
    )
    return jnp.where(same, wide, 0.0).astype(jnp.bfloat16)


def pair_rows(field_ref, block_at, shape, pair):
    tiles, slots, width, _ = shape
    reach = (slots - 1) // 2
    empty = jnp.zeros((width, width), jnp.bfloat16)
    low, high = max(2 * pair - reach, 0), min(2 * pair + reach + 2, tiles)
    lines = []
    for tile in range(low, high):
        line = [
            block_at(tile, slot_of(row - tile)) if abs(row - tile) <= reach else empty
            for row in (2 * pair, 2 * pair + 1)
        ]
        lines.append(jnp.concatenate(line, axis=1))
    source = field_ref[:, low * width : high * width]
    return jnp.dot(source, jnp.concatenate(lines, axis=0), preferred_element_type=jnp.float32)


def contribution(weight, rows):
    members, levels, columns = weight.shape
    return jnp.sum(weight.astype(jnp.float32) * rows.reshape(members, levels, columns), axis=0)


def take_rims(control_hbm, last_ref, first_ref, sems):
    rim = last_ref.shape[2]
    points = control_hbm.shape[2]
    copies = [
        pltpu.make_async_copy(control_hbm.at[:, :, pl.ds(at, rim)], ref, sems.at[i])
        for i, (at, ref) in enumerate(((points - rim, last_ref), (0, first_ref)))
    ]
    for copy in copies:
        copy.start()
    for copy in copies:
        copy.wait()


def pass_on(last_ref, first_ref, last_out, first_out):
    pass


def forward_local(loc_ref, mask_hbm, control_ref, ensemble_ref, raw_ref, inner_ref, outer_ref,
                  blocks_ref, up_ref, down_ref, edge_ref, last_ref, field_ref, mask_ref, sem):
    members, levels, points = control_ref.shape
    tiles, slots, width, _ = blocks_ref.shape
    rows, reach = members * levels, (slots - 1) // 2
    rim = reach * width
    mask_copy = pltpu.make_async_copy(mask_hbm, mask_ref, sem)
    mask_copy.start()
    up = spread(loc_ref[...], rows)
    up_ref[...] = up
    down_ref[...] = up.T
    field_ref[...] = jnp.dot(
        up, control_ref[...].reshape(rows, points), preferred_element_type=jnp.float32
    ).astype(jnp.bfloat16)
    last_ref[...] = ensemble_ref[:, :, points - rim :]
    mask_copy.wait()

    def masked(tile, slot):
        keep = mask_ref[slot, tile].astype(jnp.float32).astype(jnp.bfloat16)
        return raw_ref[tile, slot] * keep

    def kept(tile, slot):
        block = masked(tile, slot)
        blocks_ref[tile, slot] = block
        return block

    for pair in range(tiles // 2):
        columns = slice(2 * pair * width, (2 * pair + 2) * width)
        part = contribution(
            ensemble_ref[:, :, columns], pair_rows(field_ref, kept, raw_ref.shape, pair)
        )
        for i, tile in enumerate((2 * pair, 2 * pair + 1)):
            value = part[:, i * width : (i + 1) * width]
            if reach <= tile < tiles - reach:
                at = (tile - reach) * width
                inner_ref[:, at : at + width] = value.astype(jnp.bfloat16)
            else:
                at = (tile if tile < reach else tile - tiles + 2 * reach) * width
                outer_ref[:, at : at + width] = value
    empty = jnp.zeros((width, width), jnp.bfloat16)
    for side, first, source in ((0, 0, -reach), (1, tiles - reach, tiles)):
        for i in range(reach):
            for j in range(reach):
                offset = source + i - first - j
                block = empty
                if abs(offset) <= reach:
                    block = masked(first + j, slot_of(offset)).T
                edge_ref[side, i * width : (i + 1) * width, j * width : (j + 1) * width] = block


def forward_edge(left_ref, right_ref, up_ref, edge_ref, ensemble_ref, outer_ref, partial_ref):
    members, levels, points = ensemble_ref.shape
    rows, rim = members * levels, left_ref.shape[2]
    for side, ref in ((0, left_ref), (1, right_ref)):
        vertical = jnp.dot(
            up_ref[...], ref[...].reshape(rows, rim), preferred_element_type=jnp.float32
        ).astype(jnp.bfloat16)
        change = jnp.dot(vertical, edge_ref[side], preferred_element_type=jnp.float32)
        at, columns = side * (points - rim), slice(side * rim, (side + 1) * rim)
        added = contribution(ensemble_ref[:, :, at : at + rim], change)
        partial_ref[:, columns] = (outer_ref[:, columns] + added).astype(jnp.bfloat16)


def weighted(value, depart):
    members, levels, points = value.shape
    product = value.astype(jnp.float32) * depart.astype(jnp.float32)[None]
    return product.astype(jnp.bfloat16).reshape(members * levels, points)


def take_depart(inner_ref, inner_other_ref, outer_ref, outer_other_ref, background_ref,
                precision_ref, ensemble_ref, last_ref, first_ref, depart_ref, total_ref):
    rim = last_ref.shape[1]
    points = depart_ref.shape[1]
    inner = inner_ref[...].astype(jnp.float32) + inner_other_ref[...].astype(jnp.float32)
    outer = outer_ref[...].astype(jnp.float32) + outer_other_ref[...].astype(jnp.float32)
    total_ref[:, :rim] = outer[:, :rim]
    total_ref[:, rim : points - rim] = inner
    total_ref[:, points - rim :] = outer[:, rim:]
    depart_ref[...] = (precision_ref[...] * (total_ref[...] - background_ref[...])).astype(
        jnp.bfloat16
    )
    last_ref[...] = depart_ref[:, points - rim :]
    first_ref[...] = weighted(ensemble_ref[:, :, :rim], depart_ref[:, :rim])


def backward_local(depart_ref, total_ref, ensemble_ref, control_ref, blocks_ref, down_ref,
                   gradient_hbm, increment_hbm, edge_ref, field_ref, stage_ref, rows_ref, sems):
    members, levels, points = control_ref.shape
    tiles, slots, width, _ = blocks_ref.shape
    reach = (slots - 1) // 2
    rim, pairs = reach * width, tiles // 2
    place, per = lax.axis_index("mem"), rows_ref.shape[0]
    rows = total_ref[:per]
    for at in range(per, levels, per):
        rows = jnp.where(place == at // per, total_ref[at : at + per], rows)
    rows_ref[...] = rows
    copies = [pltpu.make_async_copy(rows_ref, increment_hbm, sems.at[pairs])]
    copies[0].start()
    field_ref[...] = jnp.dot(
        down_ref[...], weighted(ensemble_ref[...], depart_ref[...]),
        preferred_element_type=jnp.float32,
    ).astype(jnp.bfloat16)

    def block_at(tile, slot):
        return blocks_ref[tile, slot]

    for pair in sorted(range(pairs), key=lambda pair: -min(pair, pairs - 1 - pair)):
        at = 2 * pair * width
        change = pair_rows(field_ref, block_at, blocks_ref.shape, pair)
        control = control_ref[:, :, at : at + 2 * width].astype(jnp.float32)
        stage_ref[:, :, at : at + 2 * width] = control + change.reshape(
            members, levels, 2 * width
        )
        first, last = max(2 * pair, reach), min(2 * pair + 2, tiles - reach)
        if first < last:
            columns = pl.ds(first * width, (last - first) * width)
            copy = pltpu.make_async_copy(
                stage_ref.at[:, :, columns], gradient_hbm.at[:, :, columns], sems.at[pair]
            )
            copy.start()
            copies.append(copy)
    edge_ref[0] = stage_ref[:, :, :rim]
    edge_ref[1] = stage_ref[:, :, points - rim :]
    for copy in copies:
        copy.wait()


def backward_edge(depart_ref, right_ref, left_ref, down_ref, edge_ref, begun_ref, begun_hbm,
                  gradient_hbm, stage_ref, sems):
    members, levels, points = gradient_hbm.shape
    rim = right_ref.shape[1]
    copies = []
    for side, value in ((0, weighted(left_ref[...], depart_ref[...])), (1, right_ref[...])):
        lowered = jnp.dot(down_ref[...], value, preferred_element_type=jnp.float32)
        change = jnp.dot(
            lowered.astype(jnp.bfloat16), edge_ref[side], preferred_element_type=jnp.float32
        )
        stage_ref[side] = begun_ref[side] + change.reshape(members, levels, rim)
        columns = pl.ds(side * (points - rim), rim)
        copy = pltpu.make_async_copy(
            stage_ref.at[side], gradient_hbm.at[:, :, columns], sems.at[side]
        )
        copy.start()
        copies.append(copy)
    for copy in copies:
        copy.wait()


VMEM = pl.BlockSpec(memory_space=pltpu.VMEM)
HBM = pl.BlockSpec(memory_space=pltpu.HBM)


def call(kernel, outs, out_specs, in_specs, scratch, mib, cost, *operands, aliases=None):
    return pl.pallas_call(
        kernel,
        out_shape=outs,
        in_specs=in_specs,
        out_specs=out_specs,
        scratch_shapes=scratch,
        input_output_aliases=aliases or {},
        cost_estimate=pl.CostEstimate(flops=cost[0], bytes_accessed=cost[1], transcendentals=0),
        compiler_params=pltpu.CompilerParams(vmem_limit_bytes=mib * 2**20),
    )(*operands)


def on_device(control, ensemble, vertical_loc, blocks, edge_mask, background, obs_precision):
    members, levels, points = control.shape
    tiles, slots, width, _ = blocks.shape
    reach = (slots - 1) // 2
    rim, rows = reach * width, members * levels
    ring, group = lax.axis_size("tile"), lax.axis_size("mem")
    per = levels // group
    after = [(i, (i + 1) % ring) for i in range(ring)]
    before = [(j, i) for i, j in after]

    def half(*dims):
        return jax.ShapeDtypeStruct(dims, jnp.bfloat16)

    def single(*dims):
        return jax.ShapeDtypeStruct(dims, jnp.float32)

    def in_hbm(value):
        return pltpu.with_memory_space_constraint(value, pltpu.HBM)

    dma = pltpu.SemaphoreType.DMA
    local_flops = 2 * rows * (tiles // 2) * (2 * reach + 2) * width * 2 * width
    edge_flops = 4 * rows * rim * (rows + rim)
    sends = call(
        take_rims, [half(members, levels, rim)] * 2, [VMEM] * 2, [HBM], [dma((2,))], 2,
        (0, 8 * rows * rim), in_hbm(control),
    )
    sends = call(
        pass_on, [half(members, levels, rim)] * 2, [VMEM] * 2, [VMEM] * 2, [], 2,
        (LOADED * 10**6, LOADED * 1000), *sends, aliases={0: 0, 1: 1},
    )
    control_left = lax.ppermute(sends[0], "tile", after)
    control_right = lax.ppermute(sends[1], "tile", before)
    inner, outer, masked, up, down, edge, last = call(
        forward_local,
        [
            half(levels, points - 2 * rim), single(levels, 2 * rim), half(*blocks.shape), half(rows, rows), half(rows, rows),
            half(2, rim, rim), half(members, levels, rim),
        ],
        [VMEM] * 7,
        [VMEM, HBM, VMEM, VMEM, VMEM],
        [
            pltpu.VMEM((rows, points), jnp.bfloat16),
            pltpu.SMEM((slots, tiles), edge_mask.dtype), dma,
        ],
        16,
        (local_flops, blocks.size * 2 + 4 * control.size),
        vertical_loc, in_hbm(edge_mask.T), control, ensemble, blocks,
    )
    ensemble_left = lax.ppermute(last, "tile", after)
    outer = call(
        forward_edge, half(levels, 2 * rim), VMEM, [VMEM] * 6, [], 4,
        (edge_flops, 4 * rows * rim),
        control_left, control_right, up, edge, ensemble, outer,
    )

    def other_half(value, step):
        return lax.ppermute(value, "mem", [(i, i ^ step) for i in range(group)])

    step = 1
    while 2 * step < group:
        inner, outer = [
            (value.astype(jnp.float32) + other_half(value, step).astype(jnp.float32)).astype(
                jnp.bfloat16
            )
            for value in (inner, outer)
        ]
        step *= 2
    last, first, depart, total = call(
        take_depart,
        [half(levels, rim), half(rows, rim), half(levels, points), single(levels, points)],
        [VMEM] * 4, [VMEM] * 7, [], 4,
        (4 * levels * points, 16 * levels * points),
        inner, other_half(inner, step), outer, other_half(outer, step), background, obs_precision,
        ensemble,
    )
    depart_left = lax.ppermute(last, "tile", after)
    weighted_right = lax.ppermute(first, "tile", before)
    full = single(members, levels, points)
    gradient, increment, begun = call(
        backward_local,
        [full, single(per, points), single(2, members, levels, rim)],
        [HBM, HBM, VMEM],
        [VMEM] * 6,
        [
            pltpu.VMEM((rows, points), jnp.bfloat16),
            pltpu.VMEM((members, levels, points), jnp.float32),
            pltpu.VMEM((per, points), jnp.float32), dma((tiles // 2 + 1,)),
        ],
        8,
        (16 * local_flops, 4 * control.size),
        depart, total, ensemble, control, masked, down,
    )
    gradient = call(
        backward_edge, full, HBM, [VMEM] * 6 + [HBM],
        [pltpu.VMEM((2, members, levels, rim), jnp.float32), dma((2,))],
        4,
        (edge_flops, 4 * rows * rim),
        depart_left, weighted_right, ensemble_left, down, edge, begun, gradient,
        aliases={6: 0},
    )
    return increment, gradient


def solution(mesh):
    in_specs = (
        P("mem", None, "tile"),
        P("mem", None, "tile"),
        P(),
        P("tile", None, None, None),
        P("tile", None),
        P(None, "tile"),
        P(None, "tile"),
    )
    out_specs = (P("mem", "tile"), P("mem", None, "tile"))
    return jax.shard_map(
        on_device, mesh=mesh, in_specs=in_specs, out_specs=out_specs, check_vma=False
    )
```

```python
import jax
import jax.numpy as jnp
from jax import lax
from jax.experimental import pallas as pl
from jax.experimental.pallas import tpu as pltpu
from jax.sharding import PartitionSpec as P

LOADED = 60 * 2**20


def slot_of(offset):
    return 2 * offset - 1 if offset > 0 else -2 * offset


def spread(loc, rows):
    levels = loc.shape[0]
    pick = (
        lax.broadcasted_iota(jnp.int32, (rows, levels), 0) % levels
        == lax.broadcasted_iota(jnp.int32, (rows, levels), 1)
    ).astype(jnp.bfloat16)
    tall = jnp.concatenate([loc] * (rows // levels), axis=0)
    wide = lax.dot_general(
        tall, pick, (((1,), (1,)), ((), ())), preferred_element_type=jnp.float32
    )
    same = (
        lax.broadcasted_iota(jnp.int32, (rows, rows), 0) // levels
        == lax.broadcasted_iota(jnp.int32, (rows, rows), 1) // levels
    )
    return jnp.where(same, wide, 0.0).astype(jnp.bfloat16)


def pair_rows(field_ref, block_at, shape, pair):
    tiles, slots, width, _ = shape
    reach = (slots - 1) // 2
    empty = jnp.zeros((width, width), jnp.bfloat16)
    low, high = max(2 * pair - reach, 0), min(2 * pair + reach + 2, tiles)
    lines = []
    for tile in range(low, high):
        line = [
            block_at(tile, slot_of(row - tile)) if abs(row - tile) <= reach else empty
            for row in (2 * pair, 2 * pair + 1)
        ]
        lines.append(jnp.concatenate(line, axis=1))
    source = field_ref[:, low * width : high * width]
    return jnp.dot(source, jnp.concatenate(lines, axis=0), preferred_element_type=jnp.float32)


def contribution(weight, rows):
    members, levels, columns = weight.shape
    return jnp.sum(weight.astype(jnp.float32) * rows.reshape(members, levels, columns), axis=0)


def take_rims(control_hbm, last_ref, first_ref, sems):
    rim = last_ref.shape[2]
    points = control_hbm.shape[2]
    copies = [
        pltpu.make_async_copy(control_hbm.at[:, :, pl.ds(at, rim)], ref, sems.at[i])
        for i, (at, ref) in enumerate(((points - rim, last_ref), (0, first_ref)))
    ]
    for copy in copies:
        copy.start()
    for copy in copies:
        copy.wait()


def pass_on(last_ref, first_ref, last_out, first_out):
    pass


def forward_local(loc_ref, mask_hbm, control_ref, ensemble_ref, raw_ref, inner_ref, outer_ref,
                  blocks_ref, up_ref, down_ref, edge_ref, last_ref, field_ref, mask_ref, sem):
    members, levels, points = control_ref.shape
    tiles, slots, width, _ = blocks_ref.shape
    rows, reach = members * levels, (slots - 1) // 2
    rim = reach * width
    mask_copy = pltpu.make_async_copy(mask_hbm, mask_ref, sem)
    mask_copy.start()
    up = spread(loc_ref[...], rows)
    up_ref[...] = up
    down_ref[...] = up.T
    field_ref[...] = jnp.dot(
        up, control_ref[...].reshape(rows, points), preferred_element_type=jnp.float32
    ).astype(jnp.bfloat16)
    last_ref[...] = ensemble_ref[:, :, points - rim :]
    mask_copy.wait()

    def masked(tile, slot):
        keep = mask_ref[slot, tile].astype(jnp.float32).astype(jnp.bfloat16)
        return raw_ref[tile, slot] * keep

    def kept(tile, slot):
        block = masked(tile, slot)
        blocks_ref[tile, slot] = block
        return block

    for pair in range(tiles // 2):
        columns = slice(2 * pair * width, (2 * pair + 2) * width)
        part = contribution(
            ensemble_ref[:, :, columns], pair_rows(field_ref, kept, raw_ref.shape, pair)
        )
        for i, tile in enumerate((2 * pair, 2 * pair + 1)):
            value = part[:, i * width : (i + 1) * width]
            if reach <= tile < tiles - reach:
                at = (tile - reach) * width
                inner_ref[:, at : at + width] = value.astype(jnp.bfloat16)
            else:
                at = (tile if tile < reach else tile - tiles + 2 * reach) * width
                outer_ref[:, at : at + width] = value
    empty = jnp.zeros((width, width), jnp.bfloat16)
    for side, first, source in ((0, 0, -reach), (1, tiles - reach, tiles)):
        for i in range(reach):
            for j in range(reach):
                offset = source + i - first - j
                block = empty
                if abs(offset) <= reach:
                    block = masked(first + j, slot_of(offset)).T
                edge_ref[side, i * width : (i + 1) * width, j * width : (j + 1) * width] = block


def forward_edge(left_ref, right_ref, up_ref, edge_ref, ensemble_ref, outer_ref, partial_ref):
    members, levels, points = ensemble_ref.shape
    rows, rim = members * levels, left_ref.shape[2]
    for side, ref in ((0, left_ref), (1, right_ref)):
        vertical = jnp.dot(
            up_ref[...], ref[...].reshape(rows, rim), preferred_element_type=jnp.float32
        ).astype(jnp.bfloat16)
        change = jnp.dot(vertical, edge_ref[side], preferred_element_type=jnp.float32)
        at, columns = side * (points - rim), slice(side * rim, (side + 1) * rim)
        added = contribution(ensemble_ref[:, :, at : at + rim], change)
        partial_ref[:, columns] = (outer_ref[:, columns] + added).astype(jnp.bfloat16)


def weighted(value, depart):
    members, levels, points = value.shape
    product = value.astype(jnp.float32) * depart.astype(jnp.float32)[None]
    return product.astype(jnp.bfloat16).reshape(members * levels, points)


def fold_inner(mine_ref, other_ref, last_ref, sum_ref, last_out):
    total = mine_ref[...].astype(jnp.float32) + other_ref[...].astype(jnp.float32)
    sum_ref[...] = total.astype(jnp.bfloat16)


def depart_at(total, background_ref, precision_ref, columns):
    departed = precision_ref[:, columns] * (total - background_ref[:, columns])
    return departed.astype(jnp.bfloat16)


def take_outer(mine_ref, other_ref, background_ref, precision_ref, ensemble_ref, last_ref,
               first_ref, total_ref, depart_ref):
    rim, points = last_ref.shape[1], background_ref.shape[1]
    total = mine_ref[...].astype(jnp.float32) + other_ref[...].astype(jnp.float32)
    total_ref[...] = total
    first = depart_at(total[:, :rim], background_ref, precision_ref, slice(0, rim))
    last = depart_at(total[:, rim:], background_ref, precision_ref, slice(points - rim, points))
    depart_ref[:, :rim] = first
    depart_ref[:, rim:] = last
    last_ref[...] = last
    first_ref[...] = weighted(ensemble_ref[:, :, :rim], first)


def backward_local(outer_total_ref, outer_depart_ref, background_ref, precision_ref, inner_ref,
                   inner_other_ref, ensemble_ref, control_ref, blocks_ref, down_ref,
                   gradient_hbm, increment_hbm, edge_ref, field_ref, stage_ref, total_ref,
                   rows_ref, sems):
    members, levels, points = control_ref.shape
    tiles, slots, width, _ = blocks_ref.shape
    reach = (slots - 1) // 2
    rim, pairs = reach * width, tiles // 2
    inner = inner_ref[...].astype(jnp.float32) + inner_other_ref[...].astype(jnp.float32)
    total_ref[:, :rim] = outer_total_ref[:, :rim]
    total_ref[:, rim : points - rim] = inner
    total_ref[:, points - rim :] = outer_total_ref[:, rim:]
    depart = depart_at(inner, background_ref, precision_ref, slice(rim, points - rim))
    depart = jnp.concatenate([outer_depart_ref[:, :rim], depart, outer_depart_ref[:, rim:]], axis=1)
    place, per = lax.axis_index("mem"), rows_ref.shape[0]
    rows = total_ref[:per]
    for at in range(per, levels, per):
        rows = jnp.where(place == at // per, total_ref[at : at + per], rows)
    rows_ref[...] = rows
    copies = [pltpu.make_async_copy(rows_ref, increment_hbm, sems.at[pairs])]
    copies[0].start()
    field_ref[...] = jnp.dot(
        down_ref[...], weighted(ensemble_ref[...], depart), preferred_element_type=jnp.float32
    ).astype(jnp.bfloat16)

    def block_at(tile, slot):
        return blocks_ref[tile, slot]

    for pair in sorted(range(pairs), key=lambda pair: -min(pair, pairs - 1 - pair)):
        at = 2 * pair * width
        change = pair_rows(field_ref, block_at, blocks_ref.shape, pair)
        control = control_ref[:, :, at : at + 2 * width].astype(jnp.float32)
        stage_ref[:, :, at : at + 2 * width] = control + change.reshape(
            members, levels, 2 * width
        )
        first, last = max(2 * pair, reach), min(2 * pair + 2, tiles - reach)
        if first < last:
            columns = pl.ds(first * width, (last - first) * width)
            copy = pltpu.make_async_copy(
                stage_ref.at[:, :, columns], gradient_hbm.at[:, :, columns], sems.at[pair]
            )
            copy.start()
            copies.append(copy)
    edge_ref[0] = stage_ref[:, :, :rim]
    edge_ref[1] = stage_ref[:, :, points - rim :]
    for copy in copies:
        copy.wait()


def backward_edge(depart_ref, right_ref, left_ref, down_ref, edge_ref, begun_ref, begun_hbm,
                  gradient_hbm, stage_ref, sems):
    members, levels, points = gradient_hbm.shape
    rim = right_ref.shape[1]
    copies = []
    for side, value in ((0, weighted(left_ref[...], depart_ref[...])), (1, right_ref[...])):
        lowered = jnp.dot(down_ref[...], value, preferred_element_type=jnp.float32)
        change = jnp.dot(
            lowered.astype(jnp.bfloat16), edge_ref[side], preferred_element_type=jnp.float32
        )
        stage_ref[side] = begun_ref[side] + change.reshape(members, levels, rim)
        columns = pl.ds(side * (points - rim), rim)
        copy = pltpu.make_async_copy(
            stage_ref.at[side], gradient_hbm.at[:, :, columns], sems.at[side]
        )
        copy.start()
        copies.append(copy)
    for copy in copies:
        copy.wait()


VMEM = pl.BlockSpec(memory_space=pltpu.VMEM)
HBM = pl.BlockSpec(memory_space=pltpu.HBM)


def call(kernel, outs, out_specs, in_specs, scratch, mib, cost, *operands, aliases=None):
    return pl.pallas_call(
        kernel,
        out_shape=outs,
        in_specs=in_specs,
        out_specs=out_specs,
        scratch_shapes=scratch,
        input_output_aliases=aliases or {},
        cost_estimate=pl.CostEstimate(flops=cost[0], bytes_accessed=cost[1], transcendentals=0),
        compiler_params=pltpu.CompilerParams(vmem_limit_bytes=mib * 2**20),
    )(*operands)


def on_device(control, ensemble, vertical_loc, blocks, edge_mask, background, obs_precision):
    members, levels, points = control.shape
    tiles, slots, width, _ = blocks.shape
    reach = (slots - 1) // 2
    rim, rows = reach * width, members * levels
    ring, group = lax.axis_size("tile"), lax.axis_size("mem")
    per = levels // group
    after = [(i, (i + 1) % ring) for i in range(ring)]
    before = [(j, i) for i, j in after]

    def half(*dims):
        return jax.ShapeDtypeStruct(dims, jnp.bfloat16)

    def single(*dims):
        return jax.ShapeDtypeStruct(dims, jnp.float32)

    def in_hbm(value):
        return pltpu.with_memory_space_constraint(value, pltpu.HBM)

    dma = pltpu.SemaphoreType.DMA
    local_flops = 2 * rows * (tiles // 2) * (2 * reach + 2) * width * 2 * width
    edge_flops = 4 * rows * rim * (rows + rim)
    sends = call(
        take_rims, [half(members, levels, rim)] * 2, [VMEM] * 2, [HBM], [dma((2,))], 2,
        (0, 8 * rows * rim), in_hbm(control),
    )
    sends = call(
        pass_on, [half(members, levels, rim)] * 2, [VMEM] * 2, [VMEM] * 2, [], 2,
        (LOADED * 10**6, LOADED * 1000), *sends, aliases={0: 0, 1: 1},
    )
    control_left = lax.ppermute(sends[0], "tile", after)
    control_right = lax.ppermute(sends[1], "tile", before)
    inner, outer, masked, up, down, edge, last = call(
        forward_local,
        [
            half(levels, points - 2 * rim), single(levels, 2 * rim), half(*blocks.shape), half(rows, rows), half(rows, rows),
            half(2, rim, rim), half(members, levels, rim),
        ],
        [VMEM] * 7,
        [VMEM, HBM, VMEM, VMEM, VMEM],
        [
            pltpu.VMEM((rows, points), jnp.bfloat16),
            pltpu.SMEM((slots, tiles), edge_mask.dtype), dma,
        ],
        16,
        (local_flops, blocks.size * 2 + 4 * control.size),
        vertical_loc, in_hbm(edge_mask.T), control, ensemble, blocks,
    )
    outer = call(
        forward_edge, half(levels, 2 * rim), VMEM, [VMEM] * 6, [], 4,
        (edge_flops, 4 * rows * rim),
        control_left, control_right, up, edge, ensemble, outer,
    )

    def other_half(value, step):
        return lax.ppermute(value, "mem", [(i, i ^ step) for i in range(group)])

    step = 1
    while 2 * step < group:
        outer_other, inner_other = other_half(outer, step), other_half(inner, step)
        outer = (outer.astype(jnp.float32) + outer_other.astype(jnp.float32)).astype(jnp.bfloat16)
        inner, last = call(
            fold_inner, [half(*inner.shape), half(*last.shape)], [VMEM] * 2, [VMEM] * 3, [], 2,
            (levels * points, 6 * levels * points), inner, inner_other, last, aliases={2: 1},
        )
        step *= 2
    ensemble_left = lax.ppermute(last, "tile", after)
    outer_other, inner_other = other_half(outer, step), other_half(inner, step)
    last, first, outer, outer_depart = call(
        take_outer,
        [half(levels, rim), half(rows, rim), single(levels, 2 * rim), half(levels, 2 * rim)],
        [VMEM] * 4, [VMEM] * 5, [], 4,
        (1 * local_flops, 32 * levels * rim),
        outer, outer_other, background, obs_precision, ensemble,
    )
    depart_left = lax.ppermute(last, "tile", after)
    weighted_right = lax.ppermute(first, "tile", before)
    full = single(members, levels, points)
    gradient, increment, begun = call(
        backward_local,
        [full, single(per, points), single(2, members, levels, rim)],
        [HBM, HBM, VMEM],
        [VMEM] * 10,
        [
            pltpu.VMEM((rows, points), jnp.bfloat16),
            pltpu.VMEM((members, levels, points), jnp.float32),
            pltpu.VMEM((levels, points), jnp.float32),
            pltpu.VMEM((per, points), jnp.float32), dma((tiles // 2 + 1,)),
        ],
        8,
        (4 * local_flops, 4 * control.size),
        outer, outer_depart, background, obs_precision, inner, inner_other, ensemble, control,
        masked, down,
    )
    gradient = call(
        backward_edge, full, HBM, [VMEM] * 6 + [HBM],
        [pltpu.VMEM((2, members, levels, rim), jnp.float32), dma((2,))],
        4,
        (edge_flops, 4 * rows * rim),
        depart_left, weighted_right, ensemble_left, down, edge, begun, gradient,
        aliases={6: 0},
    )
    return increment, gradient


def solution(mesh):
    in_specs = (
        P("mem", None, "tile"),
        P("mem", None, "tile"),
        P(),
        P("tile", None, None, None),
        P("tile", None),
        P(None, "tile"),
        P(None, "tile"),
    )
    out_specs = (P("mem", "tile"), P("mem", None, "tile"))
    return jax.shard_map(
        on_device, mesh=mesh, in_specs=in_specs, out_specs=out_specs, check_vma=False
    )
```

```python
import jax
import jax.numpy as jnp
from jax import lax
from jax.experimental import pallas as pl
from jax.experimental.pallas import tpu as pltpu
from jax.sharding import PartitionSpec as P

LOADED = 60 * 2**20


def slot_of(offset):
    return 2 * offset - 1 if offset > 0 else -2 * offset


def spread(loc, rows):
    levels = loc.shape[0]
    pick = (
        lax.broadcasted_iota(jnp.int32, (rows, levels), 0) % levels
        == lax.broadcasted_iota(jnp.int32, (rows, levels), 1)
    ).astype(jnp.bfloat16)
    tall = jnp.concatenate([loc] * (rows // levels), axis=0)
    wide = lax.dot_general(
        tall, pick, (((1,), (1,)), ((), ())), preferred_element_type=jnp.float32
    )
    same = (
        lax.broadcasted_iota(jnp.int32, (rows, rows), 0) // levels
        == lax.broadcasted_iota(jnp.int32, (rows, rows), 1) // levels
    )
    return jnp.where(same, wide, 0.0).astype(jnp.bfloat16)


def pair_rows(field_ref, block_at, shape, pair):
    tiles, slots, width, _ = shape
    reach = (slots - 1) // 2
    empty = jnp.zeros((width, width), jnp.bfloat16)
    low, high = max(2 * pair - reach, 0), min(2 * pair + reach + 2, tiles)
    lines = []
    for tile in range(low, high):
        line = [
            block_at(tile, slot_of(row - tile)) if abs(row - tile) <= reach else empty
            for row in (2 * pair, 2 * pair + 1)
        ]
        lines.append(jnp.concatenate(line, axis=1))
    source = field_ref[:, low * width : high * width]
    return jnp.dot(source, jnp.concatenate(lines, axis=0), preferred_element_type=jnp.float32)


def contribution(weight, rows):
    members, levels, columns = weight.shape
    return jnp.sum(weight.astype(jnp.float32) * rows.reshape(members, levels, columns), axis=0)


def take_rims(control_hbm, last_ref, first_ref, sems):
    rim = last_ref.shape[2]
    points = control_hbm.shape[2]
    copies = [
        pltpu.make_async_copy(control_hbm.at[:, :, pl.ds(at, rim)], ref, sems.at[i])
        for i, (at, ref) in enumerate(((points - rim, last_ref), (0, first_ref)))
    ]
    for copy in copies:
        copy.start()
    for copy in copies:
        copy.wait()


def pass_on(last_ref, first_ref, last_out, first_out):
    pass


def forward_local(loc_ref, mask_hbm, control_ref, ensemble_ref, raw_ref, inner_ref, outer_ref,
                  blocks_ref, up_ref, down_ref, edge_ref, field_ref, mask_ref, sem):
    members, levels, points = control_ref.shape
    tiles, slots, width, _ = blocks_ref.shape
    rows, reach = members * levels, (slots - 1) // 2
    rim = reach * width
    mask_copy = pltpu.make_async_copy(mask_hbm, mask_ref, sem)
    mask_copy.start()
    up = spread(loc_ref[...], rows)
    up_ref[...] = up
    down_ref[...] = up.T
    field_ref[...] = jnp.dot(
        up, control_ref[...].reshape(rows, points), preferred_element_type=jnp.float32
    ).astype(jnp.bfloat16)
    mask_copy.wait()

    def masked(tile, slot):
        keep = mask_ref[slot, tile].astype(jnp.float32).astype(jnp.bfloat16)
        return raw_ref[tile, slot] * keep

    def kept(tile, slot):
        block = masked(tile, slot)
        blocks_ref[tile, slot] = block
        return block

    for pair in range(tiles // 2):
        columns = slice(2 * pair * width, (2 * pair + 2) * width)
        part = contribution(
            ensemble_ref[:, :, columns], pair_rows(field_ref, kept, raw_ref.shape, pair)
        )
        for i, tile in enumerate((2 * pair, 2 * pair + 1)):
            value = part[:, i * width : (i + 1) * width]
            if reach <= tile < tiles - reach:
                at = (tile - reach) * width
                inner_ref[:, at : at + width] = value.astype(jnp.bfloat16)
            else:
                at = (tile if tile < reach else tile - tiles + 2 * reach) * width
                outer_ref[:, at : at + width] = value
    empty = jnp.zeros((width, width), jnp.bfloat16)
    for side, first, source in ((0, 0, -reach), (1, tiles - reach, tiles)):
        for i in range(reach):
            for j in range(reach):
                offset = source + i - first - j
                block = empty
                if abs(offset) <= reach:
                    block = masked(first + j, slot_of(offset)).T
                edge_ref[side, i * width : (i + 1) * width, j * width : (j + 1) * width] = block


def forward_edge(left_ref, right_ref, up_ref, edge_ref, ensemble_ref, outer_ref, partial_ref):
    members, levels, points = ensemble_ref.shape
    rows, rim = members * levels, left_ref.shape[2]
    for side, ref in ((0, left_ref), (1, right_ref)):
        vertical = jnp.dot(
            up_ref[...], ref[...].reshape(rows, rim), preferred_element_type=jnp.float32
        ).astype(jnp.bfloat16)
        change = jnp.dot(vertical, edge_ref[side], preferred_element_type=jnp.float32)
        at, columns = side * (points - rim), slice(side * rim, (side + 1) * rim)
        added = contribution(ensemble_ref[:, :, at : at + rim], change)
        partial_ref[:, columns] = (outer_ref[:, columns] + added).astype(jnp.bfloat16)


def weighted(value, depart):
    members, levels, points = value.shape
    product = value.astype(jnp.float32) * depart.astype(jnp.float32)[None]
    return product.astype(jnp.bfloat16).reshape(members * levels, points)


def depart_at(total, background_ref, precision_ref, columns):
    departed = precision_ref[:, columns] * (total - background_ref[:, columns])
    return departed.astype(jnp.bfloat16)


def take_outer(background_ref, precision_ref, ensemble_ref, *refs):
    *part_refs, last_ref, first_ref, total_ref, depart_ref = refs
    rim, points = last_ref.shape[1], background_ref.shape[1]
    total = sum(ref[...].astype(jnp.float32) for ref in part_refs)
    total_ref[...] = total
    first = depart_at(total[:, :rim], background_ref, precision_ref, slice(0, rim))
    last = depart_at(total[:, rim:], background_ref, precision_ref, slice(points - rim, points))
    depart_ref[:, :rim] = first
    depart_ref[:, rim:] = last
    last_ref[...] = weighted(ensemble_ref[:, :, points - rim :], last)
    first_ref[...] = weighted(ensemble_ref[:, :, :rim], first)


def backward_local(outer_total_ref, outer_depart_ref, background_ref, precision_ref, inner_ref,
                   inner_other_ref, ensemble_ref, control_ref, blocks_ref, down_ref,
                   gradient_hbm, increment_hbm, edge_ref, field_ref, stage_ref, total_ref,
                   rows_ref, sems):
    members, levels, points = control_ref.shape
    tiles, slots, width, _ = blocks_ref.shape
    reach = (slots - 1) // 2
    rim, pairs = reach * width, tiles // 2
    inner = inner_ref[...].astype(jnp.float32) + inner_other_ref[...].astype(jnp.float32)
    total_ref[:, :rim] = outer_total_ref[:, :rim]
    total_ref[:, rim : points - rim] = inner
    total_ref[:, points - rim :] = outer_total_ref[:, rim:]
    depart = depart_at(inner, background_ref, precision_ref, slice(rim, points - rim))
    depart = jnp.concatenate([outer_depart_ref[:, :rim], depart, outer_depart_ref[:, rim:]], axis=1)
    place, per = lax.axis_index("mem"), rows_ref.shape[0]
    rows = total_ref[:per]
    for at in range(per, levels, per):
        rows = jnp.where(place == at // per, total_ref[at : at + per], rows)
    rows_ref[...] = rows
    copies = [pltpu.make_async_copy(rows_ref, increment_hbm, sems.at[pairs])]
    copies[0].start()
    field_ref[...] = jnp.dot(
        down_ref[...], weighted(ensemble_ref[...], depart), preferred_element_type=jnp.float32
    ).astype(jnp.bfloat16)

    def block_at(tile, slot):
        return blocks_ref[tile, slot]

    for pair in sorted(range(pairs), key=lambda pair: -min(pair, pairs - 1 - pair)):
        at = 2 * pair * width
        change = pair_rows(field_ref, block_at, blocks_ref.shape, pair)
        control = control_ref[:, :, at : at + 2 * width].astype(jnp.float32)
        stage_ref[:, :, at : at + 2 * width] = control + change.reshape(
            members, levels, 2 * width
        )
        first, last = max(2 * pair, reach), min(2 * pair + 2, tiles - reach)
        if first < last:
            columns = pl.ds(first * width, (last - first) * width)
            copy = pltpu.make_async_copy(
                stage_ref.at[:, :, columns], gradient_hbm.at[:, :, columns], sems.at[pair]
            )
            copy.start()
            copies.append(copy)
    edge_ref[0] = stage_ref[:, :, :rim]
    edge_ref[1] = stage_ref[:, :, points - rim :]
    for copy in copies:
        copy.wait()


def backward_edge(left_ref, right_ref, down_ref, edge_ref, begun_ref, begun_hbm, gradient_hbm,
                  stage_ref, sems):
    members, levels, points = gradient_hbm.shape
    rim = right_ref.shape[1]
    copies = []
    for side, ref in ((0, left_ref), (1, right_ref)):
        lowered = jnp.dot(down_ref[...], ref[...], preferred_element_type=jnp.float32)
        change = jnp.dot(
            lowered.astype(jnp.bfloat16), edge_ref[side], preferred_element_type=jnp.float32
        )
        stage_ref[side] = begun_ref[side] + change.reshape(members, levels, rim)
        columns = pl.ds(side * (points - rim), rim)
        copy = pltpu.make_async_copy(
            stage_ref.at[side], gradient_hbm.at[:, :, columns], sems.at[side]
        )
        copy.start()
        copies.append(copy)
    for copy in copies:
        copy.wait()


VMEM = pl.BlockSpec(memory_space=pltpu.VMEM)
HBM = pl.BlockSpec(memory_space=pltpu.HBM)


def call(kernel, outs, out_specs, in_specs, scratch, mib, cost, *operands, aliases=None):
    return pl.pallas_call(
        kernel,
        out_shape=outs,
        in_specs=in_specs,
        out_specs=out_specs,
        scratch_shapes=scratch,
        input_output_aliases=aliases or {},
        cost_estimate=pl.CostEstimate(flops=cost[0], bytes_accessed=cost[1], transcendentals=0),
        compiler_params=pltpu.CompilerParams(vmem_limit_bytes=mib * 2**20),
    )(*operands)


def on_device(control, ensemble, vertical_loc, blocks, edge_mask, background, obs_precision):
    members, levels, points = control.shape
    tiles, slots, width, _ = blocks.shape
    reach = (slots - 1) // 2
    rim, rows = reach * width, members * levels
    ring, group = lax.axis_size("tile"), lax.axis_size("mem")
    per = levels // group
    after = [(i, (i + 1) % ring) for i in range(ring)]
    before = [(j, i) for i, j in after]

    def half(*dims):
        return jax.ShapeDtypeStruct(dims, jnp.bfloat16)

    def single(*dims):
        return jax.ShapeDtypeStruct(dims, jnp.float32)

    def in_hbm(value):
        return pltpu.with_memory_space_constraint(value, pltpu.HBM)

    dma = pltpu.SemaphoreType.DMA
    local_flops = 2 * rows * (tiles // 2) * (2 * reach + 2) * width * 2 * width
    edge_flops = 4 * rows * rim * (rows + rim)
    sends = call(
        take_rims, [half(members, levels, rim)] * 2, [VMEM] * 2, [HBM], [dma((2,))], 2,
        (0, 8 * rows * rim), in_hbm(control),
    )
    sends = call(
        pass_on, [half(members, levels, rim)] * 2, [VMEM] * 2, [VMEM] * 2, [], 2,
        (LOADED * 10**6, LOADED * 1000), *sends, aliases={0: 0, 1: 1},
    )
    control_left = lax.ppermute(sends[0], "tile", after)
    control_right = lax.ppermute(sends[1], "tile", before)
    inner, outer, masked, up, down, edge = call(
        forward_local,
        [
            half(levels, points - 2 * rim), single(levels, 2 * rim), half(*blocks.shape), half(rows, rows), half(rows, rows),
            half(2, rim, rim),
        ],
        [VMEM] * 6,
        [VMEM, HBM, VMEM, VMEM, VMEM],
        [
            pltpu.VMEM((rows, points), jnp.bfloat16),
            pltpu.SMEM((slots, tiles), edge_mask.dtype), dma,
        ],
        16,
        (local_flops, blocks.size * 2 + 4 * control.size),
        vertical_loc, in_hbm(edge_mask.T), control, ensemble, blocks,
    )
    outer = call(
        forward_edge, half(levels, 2 * rim), VMEM, [VMEM] * 6, [], 4,
        (edge_flops, 4 * rows * rim),
        control_left, control_right, up, edge, ensemble, outer,
    )

    def other_half(value, step):
        return lax.ppermute(value, "mem", [(i, i ^ step) for i in range(group)])

    def sum_of(parts):
        return sum(part.astype(jnp.float32) for part in parts).astype(jnp.bfloat16)

    outers, done = [outer], 1
    while done < group:
        outer = sum_of(outers)
        most = min(4, group // done)
        outers = [outer] + [other_half(outer, done * i) for i in range(1, most)]
        done *= most
    step = 1
    while 2 * step < group:
        inner = sum_of([inner, other_half(inner, step)])
        step *= 2
    inner_other = other_half(inner, step)
    last, first, outer, outer_depart = call(
        take_outer,
        [half(rows, rim), half(rows, rim), single(levels, 2 * rim), half(levels, 2 * rim)],
        [VMEM] * 4, [VMEM] * (3 + len(outers)), [], 4,
        (1 * local_flops, 32 * levels * rim),
        background, obs_precision, ensemble, *outers,
    )
    weighted_left = lax.ppermute(last, "tile", after)
    weighted_right = lax.ppermute(first, "tile", before)
    full = single(members, levels, points)
    gradient, increment, begun = call(
        backward_local,
        [full, single(per, points), single(2, members, levels, rim)],
        [HBM, HBM, VMEM],
        [VMEM] * 10,
        [
            pltpu.VMEM((rows, points), jnp.bfloat16),
            pltpu.VMEM((members, levels, points), jnp.float32),
            pltpu.VMEM((levels, points), jnp.float32),
            pltpu.VMEM((per, points), jnp.float32), dma((tiles // 2 + 1,)),
        ],
        8,
        (4 * local_flops, 4 * control.size),
        outer, outer_depart, background, obs_precision, inner, inner_other, ensemble, control,
        masked, down,
    )
    gradient = call(
        backward_edge, full, HBM, [VMEM] * 5 + [HBM],
        [pltpu.VMEM((2, members, levels, rim), jnp.float32), dma((2,))],
        4,
        (edge_flops, 4 * rows * rim),
        weighted_left, weighted_right, down, edge, begun, gradient,
        aliases={5: 0},
    )
    return increment, gradient


def solution(mesh):
    in_specs = (
        P("mem", None, "tile"),
        P("mem", None, "tile"),
        P(),
        P("tile", None, None, None),
        P("tile", None),
        P(None, "tile"),
        P(None, "tile"),
    )
    out_specs = (P("mem", "tile"), P("mem", None, "tile"))
    return jax.shard_map(
        on_device, mesh=mesh, in_specs=in_specs, out_specs=out_specs, check_vma=False
    )
```

```python
import jax
import jax.numpy as jnp
from jax import lax
from jax.experimental import pallas as pl
from jax.experimental.pallas import tpu as pltpu
from jax.sharding import PartitionSpec as P

LOADED = 60 * 2**20


def slot_of(offset):
    return 2 * offset - 1 if offset > 0 else -2 * offset


def spread(loc, rows):
    levels = loc.shape[0]
    pick = (
        lax.broadcasted_iota(jnp.int32, (rows, levels), 0) % levels
        == lax.broadcasted_iota(jnp.int32, (rows, levels), 1)
    ).astype(jnp.bfloat16)
    tall = jnp.concatenate([loc] * (rows // levels), axis=0)
    wide = lax.dot_general(
        tall, pick, (((1,), (1,)), ((), ())), preferred_element_type=jnp.float32
    )
    same = (
        lax.broadcasted_iota(jnp.int32, (rows, rows), 0) // levels
        == lax.broadcasted_iota(jnp.int32, (rows, rows), 1) // levels
    )
    return jnp.where(same, wide, 0.0).astype(jnp.bfloat16)


def pair_rows(field_ref, block_at, shape, pair):
    tiles, slots, width, _ = shape
    reach = (slots - 1) // 2
    empty = jnp.zeros((width, width), jnp.bfloat16)
    low, high = max(2 * pair - reach, 0), min(2 * pair + reach + 2, tiles)
    lines = []
    for tile in range(low, high):
        line = [
            block_at(tile, slot_of(row - tile)) if abs(row - tile) <= reach else empty
            for row in (2 * pair, 2 * pair + 1)
        ]
        lines.append(jnp.concatenate(line, axis=1))
    source = field_ref[:, low * width : high * width]
    return jnp.dot(source, jnp.concatenate(lines, axis=0), preferred_element_type=jnp.float32)


def contribution(weight, rows):
    members, levels, columns = weight.shape
    return jnp.sum(weight.astype(jnp.float32) * rows.reshape(members, levels, columns), axis=0)


def take_rims(control_hbm, last_ref, first_ref, sems):
    rim = last_ref.shape[2]
    points = control_hbm.shape[2]
    copies = [
        pltpu.make_async_copy(control_hbm.at[:, :, pl.ds(at, rim)], ref, sems.at[i])
        for i, (at, ref) in enumerate(((points - rim, last_ref), (0, first_ref)))
    ]
    for copy in copies:
        copy.start()
    for copy in copies:
        copy.wait()


def pass_on(last_ref, first_ref, last_out, first_out):
    pass


def forward_local(loc_ref, mask_hbm, control_ref, ensemble_ref, raw_ref, inner_ref, outer_ref,
                  blocks_ref, up_ref, down_ref, edge_ref, last_ref, field_ref, mask_ref, sem):
    members, levels, points = control_ref.shape
    tiles, slots, width, _ = blocks_ref.shape
    rows, reach = members * levels, (slots - 1) // 2
    rim = reach * width
    mask_copy = pltpu.make_async_copy(mask_hbm, mask_ref, sem)
    mask_copy.start()
    up = spread(loc_ref[...], rows)
    up_ref[...] = up
    down_ref[...] = up.T
    field_ref[...] = jnp.dot(
        up, control_ref[...].reshape(rows, points), preferred_element_type=jnp.float32
    ).astype(jnp.bfloat16)
    last_ref[...] = ensemble_ref[:, :, points - rim :]
    mask_copy.wait()

    def masked(tile, slot):
        keep = mask_ref[slot, tile].astype(jnp.float32).astype(jnp.bfloat16)
        return raw_ref[tile, slot] * keep

    def kept(tile, slot):
        block = masked(tile, slot)
        blocks_ref[tile, slot] = block
        return block

    for pair in range(tiles // 2):
        columns = slice(2 * pair * width, (2 * pair + 2) * width)
        part = contribution(
            ensemble_ref[:, :, columns], pair_rows(field_ref, kept, raw_ref.shape, pair)
        )
        for i, tile in enumerate((2 * pair, 2 * pair + 1)):
            value = part[:, i * width : (i + 1) * width]
            if reach <= tile < tiles - reach:
                at = (tile - reach) * width
                inner_ref[:, at : at + width] = value.astype(jnp.bfloat16)
            else:
                at = (tile if tile < reach else tile - tiles + 2 * reach) * width
                outer_ref[:, at : at + width] = value
    empty = jnp.zeros((width, width), jnp.bfloat16)
    for side, first, source in ((0, 0, -reach), (1, tiles - reach, tiles)):
        for i in range(reach):
            for j in range(reach):
                offset = source + i - first - j
                block = empty
                if abs(offset) <= reach:
                    block = masked(first + j, slot_of(offset)).T
                edge_ref[side, i * width : (i + 1) * width, j * width : (j + 1) * width] = block


def forward_edge(left_ref, right_ref, up_ref, edge_ref, ensemble_ref, outer_ref, partial_ref):
    members, levels, points = ensemble_ref.shape
    rows, rim = members * levels, left_ref.shape[2]
    for side, ref in ((0, left_ref), (1, right_ref)):
        vertical = jnp.dot(
            up_ref[...], ref[...].reshape(rows, rim), preferred_element_type=jnp.float32
        ).astype(jnp.bfloat16)
        change = jnp.dot(vertical, edge_ref[side], preferred_element_type=jnp.float32)
        at, columns = side * (points - rim), slice(side * rim, (side + 1) * rim)
        added = contribution(ensemble_ref[:, :, at : at + rim], change)
        partial_ref[:, columns] = (outer_ref[:, columns] + added).astype(jnp.bfloat16)


def weighted(value, depart):
    members, levels, points = value.shape
    product = value.astype(jnp.float32) * depart.astype(jnp.float32)[None]
    return product.astype(jnp.bfloat16).reshape(members * levels, points)


def fold_inner(mine_ref, other_ref, last_ref, sum_ref, last_out):
    total = mine_ref[...].astype(jnp.float32) + other_ref[...].astype(jnp.float32)
    sum_ref[...] = total.astype(jnp.bfloat16)


def depart_at(total, background_ref, precision_ref, columns):
    departed = precision_ref[:, columns] * (total - background_ref[:, columns])
    return departed.astype(jnp.bfloat16)


def take_outer(mine_ref, other_ref, background_ref, precision_ref, ensemble_ref, last_ref,
               first_ref, total_ref, depart_ref):
    rim, points = last_ref.shape[1], background_ref.shape[1]
    total = mine_ref[...].astype(jnp.float32) + other_ref[...].astype(jnp.float32)
    total_ref[...] = total
    first = depart_at(total[:, :rim], background_ref, precision_ref, slice(0, rim))
    last = depart_at(total[:, rim:], background_ref, precision_ref, slice(points - rim, points))
    depart_ref[:, :rim] = first
    depart_ref[:, rim:] = last
    last_ref[...] = last
    first_ref[...] = weighted(ensemble_ref[:, :, :rim], first)


def backward_local(outer_total_ref, outer_depart_ref, background_ref, precision_ref, inner_ref,
                   inner_other_ref, ensemble_ref, control_ref, blocks_ref, down_ref,
                   gradient_hbm, increment_hbm, edge_ref, field_ref, stage_ref, total_ref,
                   rows_ref, sems):
    members, levels, points = control_ref.shape
    tiles, slots, width, _ = blocks_ref.shape
    reach = (slots - 1) // 2
    rim, pairs = reach * width, tiles // 2
    inner = inner_ref[...].astype(jnp.float32) + inner_other_ref[...].astype(jnp.float32)
    total_ref[:, :rim] = outer_total_ref[:, :rim]
    total_ref[:, rim : points - rim] = inner
    total_ref[:, points - rim :] = outer_total_ref[:, rim:]
    depart = depart_at(inner, background_ref, precision_ref, slice(rim, points - rim))
    depart = jnp.concatenate([outer_depart_ref[:, :rim], depart, outer_depart_ref[:, rim:]], axis=1)
    place, per = lax.axis_index("mem"), rows_ref.shape[0]
    rows = total_ref[:per]
    for at in range(per, levels, per):
        rows = jnp.where(place == at // per, total_ref[at : at + per], rows)
    rows_ref[...] = rows
    copies = [pltpu.make_async_copy(rows_ref, increment_hbm, sems.at[pairs])]
    copies[0].start()
    field_ref[...] = jnp.dot(
        down_ref[...], weighted(ensemble_ref[...], depart), preferred_element_type=jnp.float32
    ).astype(jnp.bfloat16)

    def block_at(tile, slot):
        return blocks_ref[tile, slot]

    for pair in sorted(range(pairs), key=lambda pair: -min(pair, pairs - 1 - pair)):
        at = 2 * pair * width
        change = pair_rows(field_ref, block_at, blocks_ref.shape, pair)
        control = control_ref[:, :, at : at + 2 * width].astype(jnp.float32)
        stage_ref[:, :, at : at + 2 * width] = control + change.reshape(
            members, levels, 2 * width
        )
        first, last = max(2 * pair, reach), min(2 * pair + 2, tiles - reach)
        if first < last:
            columns = pl.ds(first * width, (last - first) * width)
            copy = pltpu.make_async_copy(
                stage_ref.at[:, :, columns], gradient_hbm.at[:, :, columns], sems.at[pair]
            )
            copy.start()
            copies.append(copy)
    edge_ref[0] = stage_ref[:, :, :rim]
    edge_ref[1] = stage_ref[:, :, points - rim :]
    for copy in copies:
        copy.wait()


def backward_edge(depart_ref, right_ref, left_ref, down_ref, edge_ref, begun_ref, begun_hbm,
                  gradient_hbm, stage_ref, sems):
    members, levels, points = gradient_hbm.shape
    rim = right_ref.shape[1]
    values = (weighted(left_ref[...], depart_ref[...]), right_ref[...])
    lowered = [
        jnp.dot(down_ref[...], value, preferred_element_type=jnp.float32).astype(jnp.bfloat16)
        for value in values
    ]
    changes = [
        jnp.dot(value, edge_ref[side], preferred_element_type=jnp.float32)
        for side, value in enumerate(lowered)
    ]
    copies = []
    for side, change in enumerate(changes):
        stage_ref[side] = begun_ref[side] + change.reshape(members, levels, rim)
        columns = pl.ds(side * (points - rim), rim)
        copies.append(
            pltpu.make_async_copy(
                stage_ref.at[side], gradient_hbm.at[:, :, columns], sems.at[side]
            )
        )
    for copy in copies:
        copy.start()
    for copy in copies:
        copy.wait()


VMEM = pl.BlockSpec(memory_space=pltpu.VMEM)
HBM = pl.BlockSpec(memory_space=pltpu.HBM)


def call(kernel, outs, out_specs, in_specs, scratch, mib, cost, *operands, aliases=None):
    return pl.pallas_call(
        kernel,
        out_shape=outs,
        in_specs=in_specs,
        out_specs=out_specs,
        scratch_shapes=scratch,
        input_output_aliases=aliases or {},
        cost_estimate=pl.CostEstimate(flops=cost[0], bytes_accessed=cost[1], transcendentals=0),
        compiler_params=pltpu.CompilerParams(vmem_limit_bytes=mib * 2**20),
    )(*operands)


def on_device(control, ensemble, vertical_loc, blocks, edge_mask, background, obs_precision):
    members, levels, points = control.shape
    tiles, slots, width, _ = blocks.shape
    reach = (slots - 1) // 2
    rim, rows = reach * width, members * levels
    ring, group = lax.axis_size("tile"), lax.axis_size("mem")
    per = levels // group
    after = [(i, (i + 1) % ring) for i in range(ring)]
    before = [(j, i) for i, j in after]

    def half(*dims):
        return jax.ShapeDtypeStruct(dims, jnp.bfloat16)

    def single(*dims):
        return jax.ShapeDtypeStruct(dims, jnp.float32)

    def in_hbm(value):
        return pltpu.with_memory_space_constraint(value, pltpu.HBM)

    dma = pltpu.SemaphoreType.DMA
    local_flops = 2 * rows * (tiles // 2) * (2 * reach + 2) * width * 2 * width
    edge_flops = 4 * rows * rim * (rows + rim)
    sends = call(
        take_rims, [half(members, levels, rim)] * 2, [VMEM] * 2, [HBM], [dma((2,))], 2,
        (0, 8 * rows * rim), in_hbm(control),
    )
    sends = call(
        pass_on, [half(members, levels, rim)] * 2, [VMEM] * 2, [VMEM] * 2, [], 2,
        (LOADED * 10**6, LOADED * 1000), *sends, aliases={0: 0, 1: 1},
    )
    control_left = lax.ppermute(sends[0], "tile", after)
    control_right = lax.ppermute(sends[1], "tile", before)
    inner, outer, masked, up, down, edge, last = call(
        forward_local,
        [
            half(levels, points - 2 * rim), single(levels, 2 * rim), half(*blocks.shape), half(rows, rows), half(rows, rows),
            half(2, rim, rim), half(members, levels, rim),
        ],
        [VMEM] * 7,
        [VMEM, HBM, VMEM, VMEM, VMEM],
        [
            pltpu.VMEM((rows, points), jnp.bfloat16),
            pltpu.SMEM((slots, tiles), edge_mask.dtype), dma,
        ],
        16,
        (local_flops, blocks.size * 2 + 4 * control.size),
        vertical_loc, in_hbm(edge_mask.T), control, ensemble, blocks,
    )
    outer = call(
        forward_edge, half(levels, 2 * rim), VMEM, [VMEM] * 6, [], 4,
        (edge_flops, 4 * rows * rim),
        control_left, control_right, up, edge, ensemble, outer,
    )

    def other_half(value, step):
        return lax.ppermute(value, "mem", [(i, i ^ step) for i in range(group)])

    step = 1
    while 2 * step < group:
        outer_other, inner_other = other_half(outer, step), other_half(inner, step)
        outer = (outer.astype(jnp.float32) + outer_other.astype(jnp.float32)).astype(jnp.bfloat16)
        inner, last = call(
            fold_inner, [half(*inner.shape), half(*last.shape)], [VMEM] * 2, [VMEM] * 3, [], 2,
            (levels * points, 6 * levels * points), inner, inner_other, last, aliases={2: 1},
        )
        step *= 2
    ensemble_left = lax.ppermute(last, "tile", after)
    outer_other, inner_other = other_half(outer, step), other_half(inner, step)
    last, first, outer, outer_depart = call(
        take_outer,
        [half(levels, rim), half(rows, rim), single(levels, 2 * rim), half(levels, 2 * rim)],
        [VMEM] * 4, [VMEM] * 5, [], 4,
        (1 * local_flops, 32 * levels * rim),
        outer, outer_other, background, obs_precision, ensemble,
    )
    depart_left = lax.ppermute(last, "tile", after)
    weighted_right = lax.ppermute(first, "tile", before)
    full = single(members, levels, points)
    gradient, increment, begun = call(
        backward_local,
        [full, single(per, points), single(2, members, levels, rim)],
        [HBM, HBM, VMEM],
        [VMEM] * 10,
        [
            pltpu.VMEM((rows, points), jnp.bfloat16),
            pltpu.VMEM((members, levels, points), jnp.float32),
            pltpu.VMEM((levels, points), jnp.float32),
            pltpu.VMEM((per, points), jnp.float32), dma((tiles // 2 + 1,)),
        ],
        8,
        (4 * local_flops, 4 * control.size),
        outer, outer_depart, background, obs_precision, inner, inner_other, ensemble, control,
        masked, down,
    )
    gradient = call(
        backward_edge, full, HBM, [VMEM] * 6 + [HBM],
        [pltpu.VMEM((2, members, levels, rim), jnp.float32), dma((2,))],
        4,
        (edge_flops, 4 * rows * rim),
        depart_left, weighted_right, ensemble_left, down, edge, begun, gradient,
        aliases={6: 0},
    )
    return increment, gradient


def solution(mesh):
    in_specs = (
        P("mem", None, "tile"),
        P("mem", None, "tile"),
        P(),
        P("tile", None, None, None),
        P("tile", None),
        P(None, "tile"),
        P(None, "tile"),
    )
    out_specs = (P("mem", "tile"), P("mem", None, "tile"))
    return jax.shard_map(
        on_device, mesh=mesh, in_specs=in_specs, out_specs=out_specs, check_vma=False
    )
```
